32 devices in a mesh: groups: 2 (over y), tap: 4 (over z), tm: 2 (over x), lag: 2 (over core).
Axes of the slice: x: 2, y: 2, z: 4, core: 2. Of those that a mesh axis runs over, the one named last changes fastest.
Arguments:
- raw_strain: bfloat16 [2048, 1024], P(('groups', 'tap'), 'tm'), parts along dimension 0, may hold values from -4000 to 4000
- spatial_filter: float32 [33], replicated, may hold values from -0.35 to 0.35
- temporal_filter: float32 [255], replicated, may hold values from -0.125 to 0.125
- dest_blocks: int32 [16, 2], P('groups'), parts along dimension 0, may hold values from 0 to 7, as said below
- partner_codes: int32 [16, 128, 64], P(('groups', 'tap', 'lag'), 'tm'), parts along dimension 0, may hold values from 0 to 255, as said below
Outputs:
- coherence: bfloat16 [16, 128, 64, 512], P(('groups', 'tap', 'lag'), 'tm'), parts along dimension 0
The draws below stay inside these ranges and needn't reach their ends.
There are 2 independent parts, one for each index of `groups`. The reference program is written for one: setup_inputs(seed, part) draws one part's arguments, and reference() takes and returns one part's arrays. A program takes and returns all parts, laid end to end along the dimension named above; an argument that names none is the same for every part. Nothing has to cross between parts.
Inputs may be any that keep to these rules, and one draw needn't show every extreme that they name: With n the number of devices along lag, the values dest_blocks[s, j] // n of one row s are distinct and all differ from s // n. `partner_codes`: the 64 codes of one source tap are distinct. Within every source block, each destination slot 0 .. 1 is named by the codes of some tap of that block.
All inputs are finite; a program needn't handle non-finite values.
Results may differ from the reference program's by a relative error of at most 0.022.
Values may be sent and summed in bfloat16 or wider, within the bound.
No kernel may reach another device: no remote copies, remote signals or barrier semaphores. Data moves between devices by JAX's collectives and lax.ppermute only.
A program may use at most 128 MiB of HBM per device.

```python
import math
import jax
import jax.numpy as jnp
from jax import lax

BLOCK_TAPS = 128
PARTNERS = 64
LAG_COUNT = 512
SPACE_HALF = 16
TIME_HALF = 127
CABLE_TAPS = 1024
WINDOW = 1024
BLOCK_COUNT = 8
DEST_COUNT = 2
N_TAP = 4
N_LAG = 2


def draw_raw_strain(key, part):
    noise_key, tap_key, time_key = jax.random.split(key, 3)
    random_jitter = jnp.clip(jax.random.normal(noise_key, (CABLE_TAPS, WINDOW), jnp.float32), -6.0, 6.0)
    tap_scale = jnp.exp(jax.random.uniform(tap_key, (CABLE_TAPS, 1), jnp.float32, 0.0, math.log(10.0)))
    time_scale = jnp.exp(jax.random.uniform(time_key, (1, WINDOW), jnp.float32, 0.0, math.log(10.0)))
    strain = random_jitter * tap_scale * time_scale
    return strain.astype(jnp.bfloat16)


def draw_spatial_filter(key, part):
    sign_key, size_key = jax.random.split(key)
    length = 2 * SPACE_HALF + 1
    signs = jnp.where(jax.random.bernoulli(sign_key, 0.5, (length,)), 1.0, -1.0)
    magnitude = jax.random.uniform(size_key, (length,), jnp.float32, 0.5, 1.5)
    return (0.17 * signs * magnitude).astype(jnp.float32)


def draw_temporal_filter(key, part):
    sign_key, size_key = jax.random.split(key)
    length = 2 * TIME_HALF + 1
    signs = jnp.where(jax.random.bernoulli(sign_key, 0.5, (length,)), 1.0, -1.0)
    magnitude = jax.random.uniform(size_key, (length,), jnp.float32, 0.5, 1.5)
    return (0.06 * signs * magnitude).astype(jnp.float32)


def draw_dest_blocks(key, part):
    order_key, pick_key = jax.random.split(key)
    row_keys = jax.random.split(order_key, BLOCK_COUNT)

    def owner_pick(row_key, source):
        others = jax.random.permutation(row_key, N_TAP - 1)[:DEST_COUNT].astype(jnp.int32)
        own_owner = source // N_LAG
        return others + (others >= own_owner).astype(jnp.int32)
    owner_rows = jax.vmap(owner_pick)(row_keys, jnp.arange(BLOCK_COUNT, dtype=jnp.int32))
    lag_pick = jax.random.randint(pick_key, (BLOCK_COUNT, DEST_COUNT), 0, N_LAG, dtype=jnp.int32)
    return (owner_rows * N_LAG + lag_pick).astype(jnp.int32)


def draw_partner_codes(key, part):
    noise_key, bias_key, order_key, row_key = jax.random.split(key, 4)
    candidate_rows = DEST_COUNT * BLOCK_TAPS
    random_jitter = jax.random.randint(noise_key, (BLOCK_COUNT, BLOCK_TAPS, candidate_rows), 0, 4096, dtype=jnp.int32)
    offset_bias = jax.random.randint(bias_key, (BLOCK_COUNT, 1, DEST_COUNT, 1), 0, 2048, dtype=jnp.int32)
    offset_bias = jnp.broadcast_to(offset_bias, (BLOCK_COUNT, 1, DEST_COUNT, BLOCK_TAPS)).reshape(BLOCK_COUNT, 1, candidate_rows)
    block_keys = jax.random.split(order_key, BLOCK_COUNT)
    orders = jax.vmap(lambda block_key: jax.random.permutation(block_key, BLOCK_TAPS))(block_keys).astype(jnp.int32)
    forced_slot = orders % DEST_COUNT
    forced_row = jax.random.randint(row_key, (BLOCK_COUNT, BLOCK_TAPS), 0, BLOCK_TAPS, dtype=jnp.int32)
    forced_choice = forced_slot * BLOCK_TAPS + forced_row
    extra_reward = (jnp.arange(candidate_rows, dtype=jnp.int32)[None, None, :] == forced_choice[:, :, None]).astype(jnp.int32) * 8192
    score_values = (random_jitter + offset_bias + extra_reward) * candidate_rows + jnp.arange(candidate_rows, dtype=jnp.int32)
    best_scores, chosen = lax.top_k(score_values, PARTNERS)
    return chosen.astype(jnp.int32)


def setup_inputs(seed: int = 0, part: int = 0) -> dict:
    key_of = jax.random.split(jax.random.key(seed), 6)
    part_keys = jax.random.split(jax.random.fold_in(key_of[5], part), 6)
    return {
        "raw_strain": draw_raw_strain(jax.random.fold_in(jax.random.fold_in(key_of[5], part), 71), part),
        "spatial_filter": draw_spatial_filter(jax.random.fold_in(key_of[5], 71), part),
        "temporal_filter": draw_temporal_filter(jax.random.fold_in(key_of[5], 71), part),
        "dest_blocks": draw_dest_blocks(jax.random.fold_in(jax.random.fold_in(key_of[5], part), 71), part),
        "partner_codes": draw_partner_codes(jax.random.fold_in(jax.random.fold_in(key_of[5], part), 71), part),
    }


EPSILON = 1e-06

def reference(raw_strain, spatial_filter, temporal_filter, dest_blocks, partner_codes):
    signal = raw_strain.astype(jnp.float32)
    padded = jnp.pad(signal, ((SPACE_HALF, SPACE_HALF), (0, 0)))
    smooth = jnp.zeros_like(signal)
    for offset in range(2 * SPACE_HALF + 1):
        smooth = smooth + spatial_filter[offset] * padded[offset:offset + CABLE_TAPS]
    smooth = smooth.astype(jnp.bfloat16)
    stretched = jnp.pad(smooth.astype(jnp.float32), ((0, 0), (TIME_HALF, TIME_HALF)))

    def add_term(offset, running):
        piece = lax.dynamic_slice_in_dim(stretched, offset, WINDOW, 1)
        return running + temporal_filter[offset] * piece
    whitened = lax.fori_loop(0, 2 * TIME_HALF + 1, add_term, jnp.zeros((CABLE_TAPS, WINDOW), jnp.float32))
    whitened = whitened.astype(jnp.bfloat16)
    values = whitened.astype(jnp.float32)
    energy = lax.optimization_barrier(jnp.mean(values * values, axis=1)) + EPSILON
    length = WINDOW + LAG_COUNT
    lag_half = LAG_COUNT // 2
    spectra = jnp.fft.rfft(values, n=length, axis=1)
    code_table = partner_codes.reshape(CABLE_TAPS, PARTNERS)
    source_block = jnp.arange(CABLE_TAPS) // BLOCK_TAPS
    dest_slot = code_table // BLOCK_TAPS
    partner_tap = dest_blocks[source_block[:, None], dest_slot] * BLOCK_TAPS + code_table % BLOCK_TAPS
    energy_partner = energy[partner_tap]
    group_size = math.gcd(CABLE_TAPS, 32)
    group_count = CABLE_TAPS // group_size

    def correlate(pieces):
        source_spec, partner_index, source_energy, partner_energy = pieces
        cross_spec = jnp.conj(source_spec)[:, None, :] * spectra[partner_index]
        lagged = jnp.fft.irfft(cross_spec, n=length, axis=2)
        window_lags = jnp.concatenate([lagged[:, :, length - lag_half:], lagged[:, :, :lag_half]], axis=2)
        norm_scale = jnp.sqrt(source_energy[:, None] * partner_energy) * jnp.sqrt(jnp.float32(WINDOW))
        return (window_lags / norm_scale[:, :, None]).astype(jnp.bfloat16)
    coherence = lax.map(correlate, (spectra.reshape(group_count, group_size, -1), partner_tap.reshape(group_count, group_size, PARTNERS), energy.reshape(group_count, group_size), energy_partner.reshape(group_count, group_size, PARTNERS)))
    return coherence.reshape(BLOCK_COUNT, BLOCK_TAPS, PARTNERS, LAG_COUNT)
```

```python
import jax
import jax.numpy as jnp
from jax import lax
from jax.experimental import pallas as pl
from jax.experimental.pallas import tpu as pltpu
from jax.sharding import PartitionSpec as P

LAG_COUNT = 512
EPSILON = 1e-06
HALO = 16
TILE = 256
LANES = 128
GROUP = 8


def split_parts(matrix):
    high_part = matrix.astype(jnp.bfloat16)
    low_part = (matrix - high_part.astype(jnp.float32)).astype(jnp.bfloat16)
    return high_part, low_part


def shifted_rows(row, row_count):
    wide = jnp.broadcast_to(row, (row_count, row.shape[1]))
    return pltpu.roll(wide, 0, 1, stride=1, stride_axis=0)


def gathered(raw):
    lag_devices = lax.axis_size("lag")
    half_rows = raw.shape[0] // lag_devices
    half = lax.dynamic_slice_in_dim(raw, lax.axis_index("lag") * half_rows, half_rows, 0)

    def shifted(cells, axis, step):
        count = lax.axis_size(axis)
        return lax.ppermute(cells, axis, [(i, (i + step) % count) for i in range(count)])

    times = [half] + [shifted(half, "tm", step) for step in range(1, lax.axis_size("tm"))]
    taps = [jnp.stack(times)]
    for step in range(1, lax.axis_size("tap")):
        taps.append(jnp.stack([shifted(cells, "tap", step) for cells in times]))
    cable = jnp.stack(taps)
    return jnp.stack([cable] + [shifted(cable, "lag", step) for step in range(1, lag_devices)])


def correlate_body(
    table_ref, chosen_ref, space_ref, time_ref, cable_ref, out_ref,
    raw_ref, smooth_ref, bank_ref, flip_ref, scale_ref, picked_ref, sems,
    *, lag_devices, block_taps, time_step, dest_count, source_count, partner_count
):
    tap_devices, time_devices = cable_ref.shape[1], cable_ref.shape[2]
    time_total = time_devices * time_step
    block_total = tap_devices * lag_devices
    ext_rows = block_taps + 2 * HALO
    segments = dest_count + 1
    step_id = pl.program_id(0)
    tap_index = table_ref[segments]
    time_index = table_ref[segments + 1]
    lag_index = table_ref[segments + 2]

    def pieces(segment):
        block = table_ref[segment]
        for part, (block_at, source, target, size) in enumerate((
            (jnp.maximum(block - 1, 0), block_taps - HALO, 0, HALO),
            (block, 0, HALO, block_taps),
            (jnp.minimum(block + 1, block_total - 1), 0, HALO + block_taps, HALO),
        )):
            lag_step = lax.rem(lag_index - lax.rem(block_at, lag_devices) + lag_devices, lag_devices)
            tap_step = lax.rem(tap_index - lax.div(block_at, lag_devices) + tap_devices, tap_devices)
            for time_at in range(time_devices):
                time_step_back = lax.rem(time_index - time_at + time_devices, time_devices)
                yield pltpu.make_async_copy(
                    cable_ref.at[lag_step, tap_step, time_step_back, pl.ds(source, size)],
                    raw_ref.at[segment, pl.ds(target, size), pl.ds(time_at * time_step, time_step)],
                    sems.at[segment, part * time_devices + time_at],
                )

    @pl.when(step_id == 0)
    def prepare():
        for segment in range(segments):
            for piece in pieces(segment):
                piece.start()
        rows_at = lax.broadcasted_iota(jnp.int32, (block_taps, TILE), 1)
        space_wide = shifted_rows(space_ref[...], block_taps)[:, :ext_rows]
        time_wide = shifted_rows(time_ref[...], TILE)
        time_high, time_low = split_parts(time_wide)
        smooth_ref[:, :LANES] = jnp.zeros((segments * block_taps, LANES), jnp.bfloat16)
        smooth_ref[:, pl.ds(LANES + time_total, LANES)] = jnp.zeros(
            (segments * block_taps, LANES), jnp.bfloat16
        )
        rows_at = rows_at[:, :ext_rows]
        for segment in range(segments):
            for piece in pieces(segment):
                piece.wait()
            block = table_ref[segment]
            first = jnp.where(block == 0, HALO, 0)
            last = jnp.where(block == block_total - 1, HALO + block_taps, ext_rows)
            inside = jnp.logical_and(rows_at >= first, rows_at < last)
            space_high, space_low = split_parts(jnp.where(inside, space_wide, 0.0))
            strain = raw_ref[segment]
            smooth = jnp.dot(space_high, strain, preferred_element_type=jnp.float32)
            smooth = smooth + jnp.dot(space_low, strain, preferred_element_type=jnp.float32)
            smooth_ref[
                segment * block_taps : (segment + 1) * block_taps, pl.ds(LANES, time_total)
            ] = smooth.astype(jnp.bfloat16)
        transposed = (((1,), (1,)), ((), ()))
        dest_rows = dest_count * block_taps
        power = jnp.zeros((segments * block_taps, 1), jnp.float32)
        for tile in range(time_total // TILE):
            window = smooth_ref[:, tile * TILE : tile * TILE + 2 * TILE]
            white = lax.dot_general(
                window, time_high, transposed, preferred_element_type=jnp.float32
            )
            white = white + lax.dot_general(
                window, time_low, transposed, preferred_element_type=jnp.float32
            )
            white = white.astype(jnp.bfloat16)
            bank_ref[:, tile * TILE : (tile + 1) * TILE] = white
            white = white.astype(jnp.float32)
            power = power + jnp.sum(white * white, axis=1, keepdims=True)
        energy = power / time_total + EPSILON
        inverse = jnp.broadcast_to(1.0 / jnp.sqrt(energy), (segments * block_taps, LANES))
        inverse_high, inverse_low = split_parts(inverse)
        bank_ref[:, pl.ds(time_total, LANES)] = inverse_high
        bank_ref[:, pl.ds(time_total + LANES, LANES)] = inverse_low
        scale_ref[...] = inverse[dest_rows:]
        at_row = lax.broadcasted_iota(jnp.int32, (2 * TILE, TILE), 0)
        at_col = lax.broadcasted_iota(jnp.int32, (2 * TILE, TILE), 1)
        mirror = (at_row + at_col == TILE).astype(jnp.bfloat16)
        flip_ref[:, :LANES] = jnp.zeros((block_taps, LANES), jnp.float32)
        blank = jnp.zeros((block_taps, TILE), jnp.bfloat16)
        tiles = time_total // TILE
        for tile in range(tiles + 1):
            upper = bank_ref[dest_rows:, pl.ds((tiles - tile) * TILE, TILE)] if tile else blank
            lower = bank_ref[dest_rows:, pl.ds((tiles - tile - 1) * TILE, TILE)] if tile < tiles else blank
            turned = jnp.dot(
                jnp.concatenate([lower, upper], axis=1), mirror, preferred_element_type=jnp.float32
            )
            width = TILE if tile < tiles else LANES
            flip_ref[:, pl.ds(LANES + tile * TILE, width)] = turned[:, :width]

    dest_rows = dest_count * block_taps
    picked = jnp.dot(chosen_ref[...], bank_ref[:dest_rows, :], preferred_element_type=jnp.float32)
    picked_ref[...] = picked[:, :time_total].astype(jnp.bfloat16)
    partner_scale = picked[:, time_total : time_total + LANES] + picked[:, time_total + LANES :]
    blank = jnp.zeros((LANES, LANES), jnp.bfloat16)
    edge = jnp.zeros((partner_count, TILE), jnp.bfloat16)
    lag_tiles = LAG_COUNT // TILE
    window_scale = 1.0 / (float(time_total) ** 0.5)
    first_row = time_index * source_count + step_id * GROUP
    for member in range(GROUP):
        row = flip_ref[pl.ds(first_row + member, 1), :]
        wide = shifted_rows(row, LANES).astype(jnp.bfloat16)

        def diagonal(k):
            if k < 0 or k > time_total // LANES:
                return blank
            start = time_total + LANES - LANES * k
            return wide[:, start : start + LANES]

        weights = jnp.concatenate(
            [
                jnp.concatenate([diagonal(k), diagonal(k - 1)], axis=1)
                for k in range(2 * (time_total // TILE + lag_tiles - 1))
            ],
            axis=0,
        )
        rows = picked_ref[member * partner_count : (member + 1) * partner_count, :]
        stacked = jnp.concatenate(
            [
                jnp.concatenate([edge] * (lag_tiles - 1 - j) + [rows] + [edge] * j, axis=1)
                for j in range(lag_tiles)
            ],
            axis=0,
        )
        products = jnp.dot(stacked, weights, preferred_element_type=jnp.float32)
        scale = partner_scale[member * partner_count : (member + 1) * partner_count, :]
        scale = scale * scale_ref[pl.ds(first_row + member, 1), :] * window_scale
        scale = jnp.concatenate([scale, scale], axis=1)
        for j in range(lag_tiles):
            part = products[j * partner_count : (j + 1) * partner_count] * scale
            out_ref[0, member, :, j * TILE : (j + 1) * TILE] = part.astype(jnp.bfloat16)


def per_device(raw_strain, spatial_filter, temporal_filter, dest_blocks, partner_codes):
    taps_here, time_step = raw_strain.shape
    lag_devices = lax.axis_size("lag")
    tap_devices = lax.axis_size("tap")
    time_devices = lax.axis_size("tm")
    time_total = time_step * time_devices
    block_taps = taps_here // lag_devices
    dest_count = dest_blocks.shape[1]
    _, source_count, partner_count = partner_codes.shape
    segments = dest_count + 1
    tap_index = lax.axis_index("tap")
    time_index = lax.axis_index("tm")
    lag_index = lax.axis_index("lag")
    block_here = tap_index * lag_devices + lag_index
    cable = gathered(raw_strain)
    table = jnp.concatenate(
        [
            lax.dynamic_index_in_dim(dest_blocks, block_here, 0, keepdims=False),
            jnp.stack([block_here, tap_index, time_index, lag_index]).astype(jnp.int32),
        ]
    )
    dest_rows = dest_count * block_taps
    codes = partner_codes.reshape(source_count * partner_count, 1)
    chosen = (codes == jnp.arange(dest_rows, dtype=jnp.int32)[None, :]).astype(jnp.bfloat16)
    space_row = jnp.pad(spatial_filter, (0, TILE - spatial_filter.shape[0]))[None, :]
    time_row = jnp.pad(
        temporal_filter, (1, 2 * TILE - 1 - temporal_filter.shape[0])
    )[None, :]
    rows_all = segments * block_taps
    body = lambda *refs: correlate_body(
        *refs, lag_devices=lag_devices, block_taps=block_taps, time_step=time_step,
        dest_count=dest_count, source_count=source_count, partner_count=partner_count,
    )
    return pl.pallas_call(
        body,
        grid_spec=pltpu.PrefetchScalarGridSpec(
            num_scalar_prefetch=1,
            grid=(source_count // GROUP,),
            in_specs=[
                pl.BlockSpec((GROUP * partner_count, dest_rows), lambda i, t: (i, 0)),
                pl.BlockSpec((1, TILE), lambda i, t: (0, 0)),
                pl.BlockSpec((1, 2 * TILE), lambda i, t: (0, 0)),
                pl.BlockSpec(memory_space=pl.ANY),
            ],
            out_specs=pl.BlockSpec((1, GROUP, partner_count, LAG_COUNT), lambda i, t: (0, i, 0, 0)),
            scratch_shapes=[
                pltpu.VMEM((segments, block_taps + 2 * HALO, time_total), jnp.bfloat16),
                pltpu.VMEM((rows_all, time_total + 2 * LANES), jnp.bfloat16),
                pltpu.VMEM((rows_all, time_total + 2 * LANES), jnp.bfloat16),
                pltpu.VMEM((block_taps, time_total + 2 * LANES), jnp.float32),
                pltpu.VMEM((block_taps, LANES), jnp.float32),
                pltpu.VMEM((GROUP * partner_count, time_total), jnp.bfloat16),
                pltpu.SemaphoreType.DMA((segments, 3 * time_devices)),
            ],
        ),
        out_shape=jax.ShapeDtypeStruct((1, source_count, partner_count, LAG_COUNT), jnp.bfloat16),
        compiler_params=pltpu.CompilerParams(vmem_limit_bytes=56 << 20),
    )(table, chosen, space_row, time_row, cable)


def solution(mesh):
    placed = (
        P(("groups", "tap"), "tm"),
        P(),
        P(),
        P("groups", None),
        P(("groups", "tap", "lag"), "tm", None),
    )
    return jax.shard_map(
        per_device,
        mesh=mesh,
        in_specs=placed,
        out_specs=P(("groups", "tap", "lag"), "tm", None, None),
        check_vma=False,
    )
```

```python
import functools

import jax
import jax.numpy as jnp
from jax import lax
from jax.experimental import pallas as pl
from jax.experimental.pallas import tpu as pltpu
from jax.sharding import PartitionSpec as P

LAG_COUNT = 512
EPSILON = 1e-06
HALO = 16
TILE = 256
LANES = 128
GROUP = 16


def split_parts(matrix):
    high_part = matrix.astype(jnp.bfloat16)
    low_part = (matrix - high_part.astype(jnp.float32)).astype(jnp.bfloat16)
    return high_part, low_part


def shifted_rows(row, row_count):
    wide = jnp.broadcast_to(row, (row_count, row.shape[1]))
    return pltpu.roll(wide, 0, 1, stride=1, stride_axis=0)


def gathered(raw):
    lag_devices = lax.axis_size("lag")
    half_rows = raw.shape[0] // lag_devices
    half = lax.dynamic_slice_in_dim(raw, lax.axis_index("lag") * half_rows, half_rows, 0)

    def shifted(cells, axis, step):
        count = lax.axis_size(axis)
        return lax.ppermute(cells, axis, [(i, (i + step) % count) for i in range(count)])

    taps = [half] + [shifted(half, "tap", step) for step in range(1, lax.axis_size("tap"))]
    mine = [jnp.stack(taps)]
    for step in range(1, lax.axis_size("tm")):
        mine.append(jnp.stack([shifted(cells, "tm", step) for cells in taps]))
    cables = list(mine)
    for step in range(1, lag_devices):
        cables += [shifted(cells, "lag", step) for cells in mine]
    return cables


def correlate_body(*refs, cable_count, lag_devices, time_devices):
    dest_ref, codes_ref, space_ref, time_ref = refs[:4]
    cable_refs = refs[4 : 4 + cable_count]
    out_ref, raw_ref, smooth_ref, bank_ref, flip_ref, scale_ref, code_ref, picked_ref, sems = refs[
        4 + cable_count :
    ]
    tap_devices, block_taps, time_step = cable_refs[0].shape
    _, source_count, partner_count = codes_ref.shape
    dest_count = dest_ref.shape[1]
    dest_rows = dest_count * block_taps
    time_total = time_devices * time_step
    tiles = time_total // TILE
    block_total = tap_devices * lag_devices
    ext_rows = block_taps + 2 * HALO
    rows_all = dest_rows + source_count
    step_id = pl.program_id(0)
    tap_index = lax.axis_index("tap")
    time_index = lax.axis_index("tm")
    lag_index = lax.axis_index("lag")
    block_here = tap_index * lag_devices + lag_index

    def pieces(segment, block):
        for part, (block_at, source, target, size) in enumerate((
            (jnp.maximum(block - 1, 0), block_taps - HALO, 0, HALO),
            (block, 0, HALO, block_taps),
            (jnp.minimum(block + 1, block_total - 1), 0, HALO + block_taps, HALO),
        )):
            lag_step = lax.rem(lag_index - lax.rem(block_at, lag_devices) + lag_devices, lag_devices)
            tap_step = lax.rem(tap_index - lax.div(block_at, lag_devices) + tap_devices, tap_devices)
            for time_at in range(time_devices):
                time_back = lax.rem(time_index - time_at + time_devices, time_devices)
                cable_at = lag_step * time_devices + time_back

                def copy_from(ref):
                    return pltpu.make_async_copy(
                        ref.at[tap_step, pl.ds(source, size)],
                        raw_ref.at[
                            segment, pl.ds(target, size), pl.ds(time_at * time_step, time_step)
                        ],
                        sems.at[segment, part * time_devices + time_at],
                    )

                yield cable_at, copy_from

    def start_all(segment, block):
        for cable_at, copy_from in pieces(segment, block):
            for i, ref in enumerate(cable_refs):
                pl.when(cable_at == i)(lambda ref=ref, copy_from=copy_from: copy_from(ref).start())

    def wait_all(segment, block):
        for _, copy_from in pieces(segment, block):
            copy_from(cable_refs[0]).wait()

    @pl.when(step_id == 0)
    def prepare():
        blocks = [dest_ref[block_here, j] for j in range(dest_count)] + [block_here]
        for segment, block in enumerate(blocks):
            start_all(segment, block)
        code_ref[:, :source_count] = codes_ref[0].astype(jnp.float32).T
        space_row = jnp.pad(space_ref[...][None, :], ((0, 0), (0, TILE - space_ref.shape[0])))
        time_row = jnp.pad(time_ref[...][None, :], ((0, 0), (1, 2 * TILE - 1 - time_ref.shape[0])))
        rows_at = lax.broadcasted_iota(jnp.int32, (block_taps, ext_rows), 1)
        space_wide = shifted_rows(space_row, block_taps)[:, :ext_rows]
        time_wide = shifted_rows(time_row, TILE)
        time_high, time_low = split_parts(time_wide)
        smooth_ref[:, :LANES] = jnp.zeros((rows_all, LANES), jnp.bfloat16)
        smooth_ref[:, pl.ds(LANES + time_total, LANES)] = jnp.zeros((rows_all, LANES), jnp.bfloat16)
        for segment, block in enumerate(blocks):
            wait_all(segment, block)
            first = jnp.where(block == 0, HALO, 0)
            last = jnp.where(block == block_total - 1, HALO + block_taps, ext_rows)
            inside = jnp.logical_and(rows_at >= first, rows_at < last)
            space_high, space_low = split_parts(jnp.where(inside, space_wide, 0.0))
            strain = raw_ref[segment]
            smooth = jnp.dot(space_high, strain, preferred_element_type=jnp.float32)
            smooth = smooth + jnp.dot(space_low, strain, preferred_element_type=jnp.float32)
            smooth = smooth.astype(jnp.bfloat16)
            if segment < dest_count:
                smooth_ref[
                    segment * block_taps : (segment + 1) * block_taps, pl.ds(LANES, time_total)
                ] = smooth
            else:
                for part in range(time_devices):
                    @pl.when(time_index == part)
                    def keep_own():
                        smooth_ref[dest_rows:, pl.ds(LANES, time_total)] = smooth[
                            part * source_count : (part + 1) * source_count
                        ]
        transposed = (((1,), (1,)), ((), ()))
        power = jnp.zeros((rows_all, 1), jnp.float32)
        for tile in range(tiles):
            window = smooth_ref[:, tile * TILE : tile * TILE + 2 * TILE]
            white = lax.dot_general(
                window, time_high, transposed, preferred_element_type=jnp.float32
            )
            white = white + lax.dot_general(
                window, time_low, transposed, preferred_element_type=jnp.float32
            )
            white = white.astype(jnp.bfloat16)
            bank_ref[:, tile * TILE : (tile + 1) * TILE] = white
            white = white.astype(jnp.float32)
            power = power + jnp.sum(white * white, axis=1, keepdims=True)
        energy = power / time_total + EPSILON
        inverse = jnp.broadcast_to(1.0 / jnp.sqrt(energy), (rows_all, LANES))
        inverse_high, inverse_low = split_parts(inverse)
        bank_ref[:, pl.ds(time_total, LANES)] = inverse_high
        bank_ref[:, pl.ds(time_total + LANES, LANES)] = inverse_low
        scale_ref[...] = inverse[dest_rows:]
        at_row = lax.broadcasted_iota(jnp.int32, (2 * TILE, TILE), 0)
        at_col = lax.broadcasted_iota(jnp.int32, (2 * TILE, TILE), 1)
        mirror = (at_row + at_col == TILE).astype(jnp.bfloat16)
        flip_ref[:, :LANES] = jnp.zeros((source_count, LANES), jnp.float32)
        blank = jnp.zeros((source_count, TILE), jnp.bfloat16)
        for tile in range(tiles + 1):
            upper = bank_ref[dest_rows:, pl.ds((tiles - tile) * TILE, TILE)] if tile else blank
            lower = bank_ref[dest_rows:, pl.ds((tiles - tile - 1) * TILE, TILE)] if tile < tiles else blank
            turned = jnp.dot(
                jnp.concatenate([lower, upper], axis=1), mirror, preferred_element_type=jnp.float32
            )
            width = TILE if tile < tiles else LANES
            flip_ref[:, pl.ds(LANES + tile * TILE, width)] = turned[:, :width]

    columns = pltpu.roll(code_ref[...], lax.rem(LANES - step_id * GROUP, LANES), 1)
    at_lane = lax.broadcasted_iota(jnp.int32, (partner_count, dest_rows), 1).astype(jnp.float32)
    chosen = jnp.concatenate(
        [
            (at_lane == columns[:, member : member + 1]).astype(jnp.bfloat16)
            for member in range(GROUP)
        ],
        axis=0,
    )
    picked = jnp.dot(chosen, bank_ref[:dest_rows, :], preferred_element_type=jnp.float32)
    picked_ref[...] = picked[:, :time_total].astype(jnp.bfloat16)
    partner_scale = picked[:, time_total : time_total + LANES] + picked[:, time_total + LANES :]
    blank = jnp.zeros((LANES, LANES), jnp.bfloat16)
    window_scale = 1.0 / (float(time_total) ** 0.5)
    first_row = step_id * GROUP
    for member in range(GROUP):
        row = flip_ref[pl.ds(first_row + member, 1), :]
        wide = shifted_rows(row.astype(jnp.bfloat16), LANES)

        def diagonal(k):
            if k < 0 or k > time_total // LANES:
                return blank
            start = time_total + LANES - LANES * k
            return wide[:, start : start + LANES]

        def band(first, last):
            return jnp.concatenate(
                [
                    jnp.concatenate([diagonal(k), diagonal(k - 1)], axis=1)
                    for k in range(2 * first, 2 * last)
                ],
                axis=0,
            )

        part = slice(member * partner_count, (member + 1) * partner_count)
        rows = picked_ref[part, :]
        inner = time_total - TILE
        both = jnp.dot(
            jnp.concatenate([rows[:, :inner], rows[:, TILE:]], axis=0),
            band(1, tiles),
            preferred_element_type=jnp.float32,
        )
        before = both[:partner_count] + jnp.dot(
            rows[:, inner:], band(tiles, tiles + 1), preferred_element_type=jnp.float32
        )
        after = both[partner_count:] + jnp.dot(
            rows[:, :TILE], band(0, 1), preferred_element_type=jnp.float32
        )
        scale = partner_scale[part] * scale_ref[pl.ds(first_row + member, 1), :] * window_scale
        scale = jnp.concatenate([scale, scale], axis=1)
        out_ref[0, member, :, :TILE] = (before * scale).astype(jnp.bfloat16)
        out_ref[0, member, :, TILE:] = (after * scale).astype(jnp.bfloat16)


def per_device(raw_strain, spatial_filter, temporal_filter, dest_blocks, partner_codes):
    taps_here, time_step = raw_strain.shape
    lag_devices = lax.axis_size("lag")
    time_devices = lax.axis_size("tm")
    time_total = time_step * time_devices
    block_taps = taps_here // lag_devices
    dest_count = dest_blocks.shape[1]
    _, source_count, partner_count = partner_codes.shape
    cables = gathered(raw_strain)
    rows_all = dest_count * block_taps + source_count
    wide = time_total + 2 * LANES
    body = functools.partial(
        correlate_body,
        cable_count=len(cables),
        lag_devices=lag_devices,
        time_devices=time_devices,
    )
    return pl.pallas_call(
        body,
        grid_spec=pltpu.PrefetchScalarGridSpec(
            num_scalar_prefetch=1,
            grid=(source_count // GROUP,),
            in_specs=[
                pl.BlockSpec(partner_codes.shape, lambda i, t: (0, 0, 0)),
                pl.BlockSpec(spatial_filter.shape, lambda i, t: (0,)),
                pl.BlockSpec(temporal_filter.shape, lambda i, t: (0,)),
            ]
            + [pl.BlockSpec(memory_space=pl.ANY)] * len(cables),
            out_specs=pl.BlockSpec((1, GROUP, partner_count, LAG_COUNT), lambda i, t: (0, i, 0, 0)),
            scratch_shapes=[
                pltpu.VMEM((dest_count + 1, block_taps + 2 * HALO, time_total), jnp.bfloat16),
                pltpu.VMEM((rows_all, wide), jnp.bfloat16),
                pltpu.VMEM((rows_all, wide), jnp.bfloat16),
                pltpu.VMEM((source_count, wide), jnp.float32),
                pltpu.VMEM((source_count, LANES), jnp.float32),
                pltpu.VMEM((partner_count, LANES), jnp.float32),
                pltpu.VMEM((GROUP * partner_count, time_total), jnp.bfloat16),
                pltpu.SemaphoreType.DMA((dest_count + 1, 3 * time_devices)),
            ],
        ),
        out_shape=jax.ShapeDtypeStruct((1, source_count, partner_count, LAG_COUNT), jnp.bfloat16),
        compiler_params=pltpu.CompilerParams(vmem_limit_bytes=56 << 20),
    )(dest_blocks, partner_codes, spatial_filter, temporal_filter, *cables)


def solution(mesh):
    placed = (
        P(("groups", "tap"), "tm"),
        P(),
        P(),
        P("groups", None),
        P(("groups", "tap", "lag"), "tm", None),
    )
    return jax.shard_map(
        per_device,
        mesh=mesh,
        in_specs=placed,
        out_specs=P(("groups", "tap", "lag"), "tm", None, None),
        check_vma=False,
    )
```

```python
import functools

import jax
import jax.numpy as jnp
from jax import lax
from jax.experimental import pallas as pl
from jax.experimental.pallas import tpu as pltpu
from jax.sharding import PartitionSpec as P

LAG_COUNT = 512
EPSILON = 1e-06
HALO = 16
TILE = 256
LANES = 128
GROUP = 16
NEAR_CELLS = 2 << 20


def split_parts(matrix):
    high_part = matrix.astype(jnp.bfloat16)
    low_part = (matrix - high_part.astype(jnp.float32)).astype(jnp.bfloat16)
    return high_part, low_part


def shifted_rows(row, row_count):
    wide = jnp.broadcast_to(row, (row_count, row.shape[1]))
    return pltpu.roll(wide, 0, 1, stride=1, stride_axis=0)


def gathered(raw):
    lag_devices = lax.axis_size("lag")
    half_rows = raw.shape[0] // lag_devices
    half = lax.dynamic_slice_in_dim(raw, lax.axis_index("lag") * half_rows, half_rows, 0)

    def shifted(cells, axis, step):
        count = lax.axis_size(axis)
        return lax.ppermute(cells, axis, [(i, (i + step) % count) for i in range(count)])

    tap_devices = lax.axis_size("tap")
    taps = [half]
    for step in range(1, tap_devices // 2 + 1):
        taps.append(shifted(taps[-1], "tap", 1))
    behind = [half]
    for step in range(1, (tap_devices + 1) // 2):
        behind.append(shifted(behind[-1], "tap", tap_devices - 1))
    taps += behind[:0:-1]
    mine = [jnp.stack(taps)]
    for step in range(1, lax.axis_size("tm")):
        mine.append(jnp.stack([shifted(cells, "tm", step) for cells in taps]))
    cables = list(mine)
    for step in range(1, lag_devices):
        cables += [shifted(cells, "lag", step) for cells in mine]
    return cables


def correlate_body(*refs, cable_count, lag_devices, time_devices):
    dest_ref, codes_ref, space_ref, time_ref = refs[:4]
    cable_refs = refs[4 : 4 + cable_count]
    out_ref, raw_ref, smooth_ref, bank_ref, flip_ref, scale_ref, code_ref, picked_ref, sems = refs[
        4 + cable_count :
    ]
    tap_devices, block_taps, time_step = cable_refs[0].shape
    _, source_count, partner_count = codes_ref.shape
    dest_count = dest_ref.shape[0]
    dest_rows = dest_count * block_taps
    time_total = time_devices * time_step
    tiles = time_total // TILE
    block_total = tap_devices * lag_devices
    ext_rows = block_taps + 2 * HALO
    rows_all = dest_rows + source_count
    step_id = pl.program_id(0)
    tap_index = lax.axis_index("tap")
    time_index = lax.axis_index("tm")
    lag_index = lax.axis_index("lag")
    block_here = tap_index * lag_devices + lag_index

    def pieces(segment, block):
        for part, (block_at, source, target, size) in enumerate((
            (jnp.maximum(block - 1, 0), block_taps - HALO, 0, HALO),
            (block, 0, HALO, block_taps),
            (jnp.minimum(block + 1, block_total - 1), 0, HALO + block_taps, HALO),
        )):
            lag_step = lax.rem(lag_index - lax.rem(block_at, lag_devices) + lag_devices, lag_devices)
            tap_step = lax.rem(tap_index - lax.div(block_at, lag_devices) + tap_devices, tap_devices)
            for time_at in range(time_devices):
                time_back = lax.rem(time_index - time_at + time_devices, time_devices)
                cable_at = lag_step * time_devices + time_back

                def copy_from(ref):
                    return pltpu.make_async_copy(
                        ref.at[tap_step, pl.ds(source, size)],
                        raw_ref.at[
                            segment, pl.ds(target, size), pl.ds(time_at * time_step, time_step)
                        ],
                        sems.at[segment, part * time_devices + time_at],
                    )

                yield cable_at, copy_from

    def start_all(segment, block):
        for cable_at, copy_from in pieces(segment, block):
            for i, ref in enumerate(cable_refs):
                pl.when(cable_at == i)(lambda ref=ref, copy_from=copy_from: copy_from(ref).start())

    def wait_all(segment, block):
        for _, copy_from in pieces(segment, block):
            copy_from(cable_refs[0]).wait()

    @pl.when(step_id == 0)
    def prepare():
        blocks = [dest_ref[j, block_here] for j in range(dest_count)] + [block_here]
        for segment, block in enumerate(blocks):
            start_all(segment, block)
        code_ref[:, :source_count] = codes_ref[0].astype(jnp.float32).T
        space_row = jnp.pad(space_ref[...][None, :], ((0, 0), (0, TILE - space_ref.shape[0])))
        time_row = jnp.pad(time_ref[...][None, :], ((0, 0), (1, 2 * TILE - 1 - time_ref.shape[0])))
        rows_at = lax.broadcasted_iota(jnp.int32, (block_taps, ext_rows), 1)
        space_wide = shifted_rows(space_row, block_taps)[:, :ext_rows]
        time_wide = shifted_rows(time_row, TILE)
        time_high, time_low = split_parts(time_wide)
        smooth_ref[:, :LANES] = jnp.zeros((rows_all, LANES), jnp.bfloat16)
        smooth_ref[:, pl.ds(LANES + time_total, LANES)] = jnp.zeros((rows_all, LANES), jnp.bfloat16)
        for segment, block in enumerate(blocks):
            wait_all(segment, block)
            first = jnp.where(block == 0, HALO, 0)
            last = jnp.where(block == block_total - 1, HALO + block_taps, ext_rows)
            inside = jnp.logical_and(rows_at >= first, rows_at < last)
            space_high, space_low = split_parts(jnp.where(inside, space_wide, 0.0))
            strain = raw_ref[segment]
            smooth = jnp.dot(space_high, strain, preferred_element_type=jnp.float32)
            smooth = smooth + jnp.dot(space_low, strain, preferred_element_type=jnp.float32)
            smooth = smooth.astype(jnp.bfloat16)
            if segment < dest_count:
                smooth_ref[
                    segment * block_taps : (segment + 1) * block_taps, pl.ds(LANES, time_total)
                ] = smooth
            else:
                for part in range(time_devices):
                    @pl.when(time_index == part)
                    def keep_own():
                        smooth_ref[dest_rows:, pl.ds(LANES, time_total)] = smooth[
                            part * source_count : (part + 1) * source_count
                        ]
        transposed = (((1,), (1,)), ((), ()))
        power = jnp.zeros((rows_all, 1), jnp.float32)
        for tile in range(tiles):
            window = smooth_ref[:, tile * TILE : tile * TILE + 2 * TILE]
            white = lax.dot_general(
                window, time_high, transposed, preferred_element_type=jnp.float32
            )
            white = white + lax.dot_general(
                window, time_low, transposed, preferred_element_type=jnp.float32
            )
            white = white.astype(jnp.bfloat16)
            bank_ref[:, tile * TILE : (tile + 1) * TILE] = white
            white = white.astype(jnp.float32)
            power = power + jnp.sum(white * white, axis=1, keepdims=True)
        energy = power / time_total + EPSILON
        inverse = jnp.broadcast_to(1.0 / jnp.sqrt(energy), (rows_all, LANES))
        inverse_high, inverse_low = split_parts(inverse)
        bank_ref[:, pl.ds(time_total, LANES)] = inverse_high
        bank_ref[:, pl.ds(time_total + LANES, LANES)] = inverse_low
        scale_ref[...] = inverse[dest_rows:]
        at_row = lax.broadcasted_iota(jnp.int32, (2 * TILE, TILE), 0)
        at_col = lax.broadcasted_iota(jnp.int32, (2 * TILE, TILE), 1)
        mirror = (at_row + at_col == TILE).astype(jnp.bfloat16)
        flip_ref[:, :LANES] = jnp.zeros((source_count, LANES), jnp.float32)
        blank = jnp.zeros((source_count, TILE), jnp.bfloat16)
        for tile in range(tiles + 1):
            upper = bank_ref[dest_rows:, pl.ds((tiles - tile) * TILE, TILE)] if tile else blank
            lower = bank_ref[dest_rows:, pl.ds((tiles - tile - 1) * TILE, TILE)] if tile < tiles else blank
            turned = jnp.dot(
                jnp.concatenate([lower, upper], axis=1), mirror, preferred_element_type=jnp.float32
            )
            width = TILE if tile < tiles else LANES
            flip_ref[:, pl.ds(LANES + tile * TILE, width)] = turned[:, :width]

    columns = pltpu.roll(code_ref[...], lax.rem(LANES - step_id * GROUP, LANES), 1)
    at_lane = lax.broadcasted_iota(jnp.int32, (partner_count, dest_rows), 1).astype(jnp.float32)
    chosen = jnp.concatenate(
        [
            (at_lane == columns[:, member : member + 1]).astype(jnp.bfloat16)
            for member in range(GROUP)
        ],
        axis=0,
    )
    picked = jnp.dot(chosen, bank_ref[:dest_rows, :], preferred_element_type=jnp.float32)
    picked_ref[...] = picked[:, :time_total].astype(jnp.bfloat16)
    partner_scale = picked[:, time_total : time_total + LANES] + picked[:, time_total + LANES :]
    blank = jnp.zeros((LANES, LANES), jnp.bfloat16)
    window_scale = 1.0 / (float(time_total) ** 0.5)
    first_row = step_id * GROUP
    for member in range(GROUP):
        row = flip_ref[pl.ds(first_row + member, 1), :]
        wide = shifted_rows(row.astype(jnp.bfloat16), LANES)

        def diagonal(k):
            if k < 0 or k > time_total // LANES:
                return blank
            start = time_total + LANES - LANES * k
            return wide[:, start : start + LANES]

        def band(first, last):
            return jnp.concatenate(
                [
                    jnp.concatenate([diagonal(k), diagonal(k - 1)], axis=1)
                    for k in range(2 * first, 2 * last)
                ],
                axis=0,
            )

        part = slice(member * partner_count, (member + 1) * partner_count)
        rows = picked_ref[part, :]
        inner = time_total - TILE
        both = jnp.dot(
            jnp.concatenate([rows[:, :inner], rows[:, TILE:]], axis=0),
            band(1, tiles),
            preferred_element_type=jnp.float32,
        )
        before = both[:partner_count] + jnp.dot(
            rows[:, inner:], band(tiles, tiles + 1), preferred_element_type=jnp.float32
        )
        after = both[partner_count:] + jnp.dot(
            rows[:, :TILE], band(0, 1), preferred_element_type=jnp.float32
        )
        scale = partner_scale[part] * scale_ref[pl.ds(first_row + member, 1), :] * window_scale
        scale = jnp.concatenate([scale, scale], axis=1)
        out_ref[0, member, :, :TILE] = (before * scale).astype(jnp.bfloat16)
        out_ref[0, member, :, TILE:] = (after * scale).astype(jnp.bfloat16)


def per_device(raw_strain, spatial_filter, temporal_filter, dest_blocks, partner_codes):
    taps_here, time_step = raw_strain.shape
    lag_devices = lax.axis_size("lag")
    time_devices = lax.axis_size("tm")
    time_total = time_step * time_devices
    block_taps = taps_here // lag_devices
    dest_count = dest_blocks.shape[1]
    _, source_count, partner_count = partner_codes.shape
    cables = gathered(raw_strain)
    near = sum(cells.size for cells in cables) <= NEAR_CELLS
    if near:
        cables = [pltpu.with_memory_space_constraint(cells, pltpu.VMEM) for cells in cables]
    rows_all = dest_count * block_taps + source_count
    wide = time_total + 2 * LANES
    body = functools.partial(
        correlate_body,
        cable_count=len(cables),
        lag_devices=lag_devices,
        time_devices=time_devices,
    )
    return pl.pallas_call(
        body,
        grid_spec=pltpu.PrefetchScalarGridSpec(
            num_scalar_prefetch=1,
            grid=(source_count // GROUP,),
            in_specs=[
                pl.BlockSpec(partner_codes.shape, lambda i, t: (0, 0, 0)),
                pl.BlockSpec(spatial_filter.shape, lambda i, t: (0,)),
                pl.BlockSpec(temporal_filter.shape, lambda i, t: (0,)),
            ]
            + [pl.BlockSpec(memory_space=pltpu.VMEM if near else pl.ANY)] * len(cables),
            out_specs=pl.BlockSpec((1, GROUP, partner_count, LAG_COUNT), lambda i, t: (0, i, 0, 0)),
            scratch_shapes=[
                pltpu.VMEM((dest_count + 1, block_taps + 2 * HALO, time_total), jnp.bfloat16),
                pltpu.VMEM((rows_all, wide), jnp.bfloat16),
                pltpu.VMEM((rows_all, wide), jnp.bfloat16),
                pltpu.VMEM((source_count, wide), jnp.float32),
                pltpu.VMEM((source_count, LANES), jnp.float32),
                pltpu.VMEM((partner_count, LANES), jnp.float32),
                pltpu.VMEM((GROUP * partner_count, time_total), jnp.bfloat16),
                pltpu.SemaphoreType.DMA((dest_count + 1, 3 * time_devices)),
            ],
        ),
        out_shape=jax.ShapeDtypeStruct((1, source_count, partner_count, LAG_COUNT), jnp.bfloat16),
        compiler_params=pltpu.CompilerParams(vmem_limit_bytes=56 << 20),
    )(dest_blocks.T, partner_codes, spatial_filter, temporal_filter, *cables)


def solution(mesh):
    placed = (
        P(("groups", "tap"), "tm"),
        P(),
        P(),
        P("groups", None),
        P(("groups", "tap", "lag"), "tm", None),
    )
    return jax.shard_map(
        per_device,
        mesh=mesh,
        in_specs=placed,
        out_specs=P(("groups", "tap", "lag"), "tm", None, None),
        check_vma=False,
    )
```

```python
import functools

import jax
import jax.numpy as jnp
from jax import lax
from jax.experimental import pallas as pl
from jax.experimental.pallas import tpu as pltpu
from jax.sharding import PartitionSpec as P

LAG_COUNT = 512
EPSILON = 1e-06
HALO = 16
TILE = 256
LANES = 128
GROUP = 16
NEAR_CELLS = 2 << 20


def split_parts(matrix):
    high_part = matrix.astype(jnp.bfloat16)
    low_part = (matrix - high_part.astype(jnp.float32)).astype(jnp.bfloat16)
    return high_part, low_part


def shifted_rows(row, row_count):
    wide = jnp.broadcast_to(row, (row_count, row.shape[1]))
    return pltpu.roll(wide, 0, 1, stride=1, stride_axis=0)


def gathered(raw, bands):
    lag_devices = lax.axis_size("lag")
    half_rows = raw.shape[0] // lag_devices
    half = lax.dynamic_slice_in_dim(raw, lax.axis_index("lag") * half_rows, half_rows, 0)

    def shifted(cells, axis, step):
        count = lax.axis_size(axis)
        return lax.ppermute(cells, axis, [(i, (i + step) % count) for i in range(count)])

    tap_devices = lax.axis_size("tap")
    ahead, behind = [half], [half]
    for step in range(1, tap_devices // 2 + 1):
        ahead.append(shifted(ahead[-1], "tap", 1))
        if step == 1:
            ahead[1], *bands = lax.optimization_barrier((ahead[1], *bands))
    for step in range(1, (tap_devices + 1) // 2):
        behind.append(shifted(behind[-1], "tap", tap_devices - 1))
    taps = ahead + behind[:0:-1]
    mine = [None]
    for step in range(1, lax.axis_size("tm")):
        swapped = shifted(half, "tm", step)
        if step == 1 and tap_devices > 2:
            taps[2], swapped = lax.optimization_barrier((taps[2], swapped))
        mine.append(jnp.stack([swapped] + [shifted(cells, "tm", step) for cells in taps[1:]]))
    mine[0] = jnp.stack(taps)
    cables = list(mine)
    for step in range(1, lag_devices):
        cables += [shifted(cells, "lag", step) for cells in mine]
    return cables, bands


def bands_body(dest_ref, codes_ref, space_ref, time_ref, space_out, time_out, code_out, *, block_total):
    _, source_count, partner_count = codes_ref.shape
    rows_all, ext_rows = space_out.shape[1:]
    dest_count = dest_ref.shape[0]
    block_taps = ext_rows - 2 * HALO
    tap_index = lax.axis_index("tap")
    time_index = lax.axis_index("tm")
    block_here = tap_index * lax.axis_size("lag") + lax.axis_index("lag")
    code_out[:, :source_count] = codes_ref[0].astype(jnp.float32).T
    space_row = jnp.pad(space_ref[...][None, :], ((0, 0), (0, TILE - space_ref.shape[0])))
    for segment in range(dest_count + 1):
        own = segment == dest_count
        block = block_here if own else dest_ref[segment, block_here]
        row_count = source_count if own else block_taps
        wide = shifted_rows(space_row, row_count)
        if own:
            wide = pltpu.roll(wide, time_index * source_count, 1)
        rows_at = lax.broadcasted_iota(jnp.int32, (row_count, ext_rows), 1)
        first = jnp.where(block == 0, HALO, 0)
        last = jnp.where(block == block_total - 1, HALO + block_taps, ext_rows)
        inside = jnp.logical_and(rows_at >= first, rows_at < last)
        high, low = split_parts(jnp.where(inside, wide[:, :ext_rows], 0.0))
        rows = slice(segment * block_taps, segment * block_taps + row_count)
        space_out[0, rows, :] = high
        space_out[1, rows, :] = low
    time_row = jnp.pad(time_ref[...][None, :], ((0, 0), (1, 2 * TILE - 1 - time_ref.shape[0])))
    high, low = split_parts(shifted_rows(time_row, TILE).T)
    time_out[0] = high
    time_out[1] = low


def correlate_body(*refs, near, cable_count, lag_devices, time_devices):
    dest_ref, space_ref, time_ref, code_ref = refs[:4]
    cable_refs = refs[4 : 4 + cable_count]
    out_ref, raw_ref, smooth_ref, bank_ref, flip_ref, scale_ref, picked_ref, sems = refs[
        4 + cable_count :
    ]
    tap_devices, block_taps, time_step = cable_refs[0].shape
    source_count, partner_count = flip_ref.shape[0], code_ref.shape[0]
    dest_count = dest_ref.shape[0]
    dest_rows = dest_count * block_taps
    time_total = time_devices * time_step
    tiles = time_total // TILE
    block_total = tap_devices * lag_devices
    ext_rows = block_taps + 2 * HALO
    rows_all = dest_rows + source_count
    step_id = pl.program_id(0)
    tap_index = lax.axis_index("tap")
    time_index = lax.axis_index("tm")
    lag_index = lax.axis_index("lag")
    block_here = tap_index * lag_devices + lag_index

    def pieces(segment, block):
        for part, (block_at, source, target, size) in enumerate((
            (jnp.maximum(block - 1, 0), block_taps - HALO, 0, HALO),
            (block, 0, HALO, block_taps),
            (jnp.minimum(block + 1, block_total - 1), 0, HALO + block_taps, HALO),
        )):
            lag_step = lax.rem(lag_index - lax.rem(block_at, lag_devices) + lag_devices, lag_devices)
            tap_step = lax.rem(tap_index - lax.div(block_at, lag_devices) + tap_devices, tap_devices)
            for time_at in range(time_devices):
                time_back = lax.rem(time_index - time_at + time_devices, time_devices)
                cable_at = lag_step * time_devices + time_back

                def copy_from(
                    ref, wait=False, tap_step=tap_step, part=part, time_at=time_at,
                    source=source, target=target, size=size,
                ):
                    times = pl.ds(time_at * time_step, time_step)
                    if near:
                        raw_ref[segment, pl.ds(target, size), times] = ref[
                            tap_step, pl.ds(source, size)
                        ]
                        return
                    copy = pltpu.make_async_copy(
                        ref.at[tap_step, pl.ds(source, size)],
                        raw_ref.at[segment, pl.ds(target, size), times],
                        sems.at[segment, part * time_devices + time_at],
                    )
                    copy.wait() if wait else copy.start()

                yield cable_at, copy_from

    def start_all(segment, block):
        for cable_at, copy_from in pieces(segment, block):
            for i, ref in enumerate(cable_refs):
                pl.when(cable_at == i)(lambda ref=ref, copy_from=copy_from: copy_from(ref))

    def wait_all(segment, block):
        if not near:
            for _, copy_from in pieces(segment, block):
                copy_from(cable_refs[0], wait=True)

    @pl.when(step_id == 0)
    def prepare():
        blocks = [dest_ref[j, block_here] for j in range(dest_count)] + [block_here]
        for segment, block in enumerate(blocks):
            start_all(segment, block)
        smooth_ref[:, :LANES] = jnp.zeros((rows_all, LANES), jnp.bfloat16)
        smooth_ref[:, pl.ds(LANES + time_total, LANES)] = jnp.zeros((rows_all, LANES), jnp.bfloat16)
        for segment, block in enumerate(blocks):
            wait_all(segment, block)
            first = segment * block_taps
            rows = slice(first, first + (block_taps if segment < dest_count else source_count))
            strain = raw_ref[segment]
            smooth = jnp.dot(space_ref[0, rows], strain, preferred_element_type=jnp.float32)
            smooth = smooth + jnp.dot(
                space_ref[1, rows], strain, preferred_element_type=jnp.float32
            )
            smooth_ref[rows, pl.ds(LANES, time_total)] = smooth.astype(jnp.bfloat16)
        power = jnp.zeros((rows_all, 1), jnp.float32)
        for tile in range(tiles):
            window = smooth_ref[:, tile * TILE : tile * TILE + 2 * TILE]
            white = jnp.dot(window, time_ref[0], preferred_element_type=jnp.float32)
            white = white + jnp.dot(window, time_ref[1], preferred_element_type=jnp.float32)
            white = white.astype(jnp.bfloat16)
            bank_ref[:, tile * TILE : (tile + 1) * TILE] = white
            white = white.astype(jnp.float32)
            power = power + jnp.sum(white * white, axis=1, keepdims=True)
        energy = power / time_total + EPSILON
        inverse = jnp.broadcast_to(1.0 / jnp.sqrt(energy), (rows_all, LANES))
        inverse_high, inverse_low = split_parts(inverse)
        bank_ref[:, pl.ds(time_total, LANES)] = inverse_high
        bank_ref[:, pl.ds(time_total + LANES, LANES)] = inverse_low
        scale_ref[...] = inverse[dest_rows:]
        at_row = lax.broadcasted_iota(jnp.int32, (2 * TILE, TILE), 0)
        at_col = lax.broadcasted_iota(jnp.int32, (2 * TILE, TILE), 1)
        mirror = (at_row + at_col == TILE).astype(jnp.bfloat16)
        flip_ref[:, :LANES] = jnp.zeros((source_count, LANES), jnp.float32)
        blank = jnp.zeros((source_count, TILE), jnp.bfloat16)
        for tile in range(tiles + 1):
            upper = bank_ref[dest_rows:, pl.ds((tiles - tile) * TILE, TILE)] if tile else blank
            lower = bank_ref[dest_rows:, pl.ds((tiles - tile - 1) * TILE, TILE)] if tile < tiles else blank
            turned = jnp.dot(
                jnp.concatenate([lower, upper], axis=1), mirror, preferred_element_type=jnp.float32
            )
            width = TILE if tile < tiles else LANES
            flip_ref[:, pl.ds(LANES + tile * TILE, width)] = turned[:, :width]

    columns = pltpu.roll(code_ref[...], lax.rem(LANES - step_id * GROUP, LANES), 1)
    at_lane = lax.broadcasted_iota(jnp.int32, (partner_count, dest_rows), 1).astype(jnp.float32)
    chosen = jnp.concatenate(
        [
            (at_lane == columns[:, member : member + 1]).astype(jnp.bfloat16)
            for member in range(GROUP)
        ],
        axis=0,
    )
    picked = jnp.dot(chosen, bank_ref[:dest_rows, :], preferred_element_type=jnp.float32)
    picked_ref[...] = picked[:, :time_total].astype(jnp.bfloat16)
    partner_scale = picked[:, time_total : time_total + LANES] + picked[:, time_total + LANES :]
    blank = jnp.zeros((LANES, LANES), jnp.bfloat16)
    window_scale = 1.0 / (float(time_total) ** 0.5)
    first_row = step_id * GROUP
    for member in range(GROUP):
        row = flip_ref[pl.ds(first_row + member, 1), :]
        wide = shifted_rows(row.astype(jnp.bfloat16), LANES)

        def diagonal(k):
            if k < 0 or k > time_total // LANES:
                return blank
            start = time_total + LANES - LANES * k
            return wide[:, start : start + LANES]

        def band(first, last):
            return jnp.concatenate(
                [
                    jnp.concatenate([diagonal(k), diagonal(k - 1)], axis=1)
                    for k in range(2 * first, 2 * last)
                ],
                axis=0,
            )

        part = slice(member * partner_count, (member + 1) * partner_count)
        rows = picked_ref[part, :]
        edge = jnp.zeros((partner_count, TILE), jnp.bfloat16)
        both = jnp.dot(
            jnp.concatenate(
                [jnp.concatenate([edge, rows], axis=1), jnp.concatenate([rows, edge], axis=1)],
                axis=0,
            ),
            band(0, tiles + 1),
            preferred_element_type=jnp.float32,
        )
        before, after = both[:partner_count], both[partner_count:]
        scale = partner_scale[part] * scale_ref[pl.ds(first_row + member, 1), :] * window_scale
        scale = jnp.concatenate([scale, scale], axis=1)
        out_ref[0, member, :, :TILE] = (before * scale).astype(jnp.bfloat16)
        out_ref[0, member, :, TILE:] = (after * scale).astype(jnp.bfloat16)


def per_device(raw_strain, spatial_filter, temporal_filter, dest_blocks, partner_codes):
    taps_here, time_step = raw_strain.shape
    lag_devices = lax.axis_size("lag")
    time_devices = lax.axis_size("tm")
    time_total = time_step * time_devices
    block_taps = taps_here // lag_devices
    dest_count = dest_blocks.shape[1]
    _, source_count, partner_count = partner_codes.shape
    rows_all = dest_count * block_taps + source_count
    placed = pl.BlockSpec(memory_space=pltpu.VMEM)
    bands = pl.pallas_call(
        functools.partial(bands_body, block_total=dest_blocks.shape[0]),
        grid_spec=pltpu.PrefetchScalarGridSpec(
            num_scalar_prefetch=1,
            grid=(),
            in_specs=[placed] * 3,
            out_specs=[placed] * 3,
        ),
        out_shape=[
            pltpu.VMEM((2, rows_all, block_taps + 2 * HALO), jnp.bfloat16),
            pltpu.VMEM((2, 2 * TILE, TILE), jnp.bfloat16),
            pltpu.VMEM((partner_count, LANES), jnp.float32),
        ],
    )(dest_blocks.T, partner_codes, spatial_filter, temporal_filter)
    cables, bands = gathered(raw_strain, bands)
    bands = [pltpu.with_memory_space_constraint(band, pltpu.VMEM) for band in bands]
    near = sum(cells.size for cells in cables) <= NEAR_CELLS
    if near:
        cables = [pltpu.with_memory_space_constraint(cells, pltpu.VMEM) for cells in cables]
    wide = time_total + 2 * LANES
    body = functools.partial(
        correlate_body,
        near=near,
        cable_count=len(cables),
        lag_devices=lag_devices,
        time_devices=time_devices,
    )
    return pl.pallas_call(
        body,
        grid_spec=pltpu.PrefetchScalarGridSpec(
            num_scalar_prefetch=1,
            grid=(source_count // GROUP,),
            in_specs=[placed] * 3 + [placed if near else pl.BlockSpec(memory_space=pl.ANY)] * len(cables),
            out_specs=pl.BlockSpec((1, GROUP, partner_count, LAG_COUNT), lambda i, t: (0, i, 0, 0)),
            scratch_shapes=[
                pltpu.VMEM((dest_count + 1, block_taps + 2 * HALO, time_total), jnp.bfloat16),
                pltpu.VMEM((rows_all, wide), jnp.bfloat16),
                pltpu.VMEM((rows_all, wide), jnp.bfloat16),
                pltpu.VMEM((source_count, wide), jnp.float32),
                pltpu.VMEM((source_count, LANES), jnp.float32),
                pltpu.VMEM((GROUP * partner_count, time_total), jnp.bfloat16),
                pltpu.SemaphoreType.DMA((dest_count + 1, 3 * time_devices)),
            ],
        ),
        out_shape=jax.ShapeDtypeStruct((1, source_count, partner_count, LAG_COUNT), jnp.bfloat16),
        compiler_params=pltpu.CompilerParams(vmem_limit_bytes=56 << 20),
    )(dest_blocks.T, *bands, *cables)


def solution(mesh):
    placed = (
        P(("groups", "tap"), "tm"),
        P(),
        P(),
        P("groups", None),
        P(("groups", "tap", "lag"), "tm", None),
    )
    return jax.shard_map(
        per_device,
        mesh=mesh,
        in_specs=placed,
        out_specs=P(("groups", "tap", "lag"), "tm", None, None),
        check_vma=False,
    )
```

```python
import functools

import jax
import jax.numpy as jnp
from jax import lax
from jax.experimental import pallas as pl
from jax.experimental.pallas import tpu as pltpu
from jax.sharding import PartitionSpec as P

LAG_COUNT = 512
EPSILON = 1e-06
HALO = 16
TILE = 256
LANES = 128
GROUP = 32
CHUNK = 4
NEAR_CELLS = 2 << 20


def split_parts(matrix):
    high_part = matrix.astype(jnp.bfloat16)
    low_part = (matrix - high_part.astype(jnp.float32)).astype(jnp.bfloat16)
    return high_part, low_part


def shifted_rows(row, row_count):
    wide = jnp.broadcast_to(row, (row_count, row.shape[1]))
    return pltpu.roll(wide, 0, 1, stride=1, stride_axis=0)


def gathered(raw, bands):
    lag_devices = lax.axis_size("lag")
    half_rows = raw.shape[0] // lag_devices
    half = lax.dynamic_slice_in_dim(raw, lax.axis_index("lag") * half_rows, half_rows, 0)

    def shifted(cells, axis, step):
        count = lax.axis_size(axis)
        return lax.ppermute(cells, axis, [(i, (i + step) % count) for i in range(count)])

    tap_devices = lax.axis_size("tap")
    ahead, behind = [half], [half]
    for step in range(1, tap_devices // 2 + 1):
        ahead.append(shifted(ahead[-1], "tap", 1))
        if step == 1:
            ahead[1], *bands = lax.optimization_barrier((ahead[1], *bands))
    for step in range(1, (tap_devices + 1) // 2):
        behind.append(shifted(behind[-1], "tap", tap_devices - 1))
    taps = ahead + behind[:0:-1]
    mine = [None]
    for step in range(1, lax.axis_size("tm")):
        swapped = shifted(half, "tm", step)
        if step == 1 and tap_devices > 2:
            taps[2], swapped = lax.optimization_barrier((taps[2], swapped))
        mine.append(jnp.stack([swapped] + [shifted(cells, "tm", step) for cells in taps[1:]]))
    mine[0] = jnp.stack(taps)
    cables = list(mine)
    for step in range(1, lag_devices):
        cables += [shifted(cells, "lag", step) for cells in mine]
    return cables, bands


def bands_body(dest_ref, codes_ref, space_ref, time_ref, space_out, time_out, code_out, *, block_total):
    _, source_count, partner_count = codes_ref.shape
    rows_all, ext_rows = space_out.shape[1:]
    dest_count = dest_ref.shape[0]
    block_taps = ext_rows - 2 * HALO
    tap_index = lax.axis_index("tap")
    time_index = lax.axis_index("tm")
    block_here = tap_index * lax.axis_size("lag") + lax.axis_index("lag")
    code_out[:, :source_count] = codes_ref[0].astype(jnp.float32).T
    space_row = jnp.pad(space_ref[...][None, :], ((0, 0), (0, TILE - space_ref.shape[0])))
    for segment in range(dest_count + 1):
        own = segment == dest_count
        block = block_here if own else dest_ref[segment, block_here]
        row_count = source_count if own else block_taps
        wide = shifted_rows(space_row, row_count)
        if own:
            wide = pltpu.roll(wide, time_index * source_count, 1)
        rows_at = lax.broadcasted_iota(jnp.int32, (row_count, ext_rows), 1)
        first = jnp.where(block == 0, HALO, 0)
        last = jnp.where(block == block_total - 1, HALO + block_taps, ext_rows)
        inside = jnp.logical_and(rows_at >= first, rows_at < last)
        high, low = split_parts(jnp.where(inside, wide[:, :ext_rows], 0.0))
        rows = slice(segment * block_taps, segment * block_taps + row_count)
        space_out[0, rows, :] = high
        space_out[1, rows, :] = low
    time_row = jnp.pad(time_ref[...][None, :], ((0, 0), (1, 2 * TILE - 1 - time_ref.shape[0])))
    high, low = split_parts(shifted_rows(time_row, TILE).T)
    time_out[0] = high
    time_out[1] = low


def correlate_body(*refs, near, cable_count, lag_devices, time_devices):
    dest_ref, space_ref, time_ref, code_ref = refs[:4]
    cable_refs = refs[4 : 4 + cable_count]
    out_ref, raw_ref, smooth_ref, bank_ref, flip_ref, scale_ref, partner_ref, picked_ref, sems = refs[
        4 + cable_count :
    ]
    tap_devices, block_taps, time_step = cable_refs[0].shape
    source_count, partner_count = flip_ref.shape[0], code_ref.shape[0]
    dest_count = dest_ref.shape[0]
    dest_rows = dest_count * block_taps
    time_total = time_devices * time_step
    tiles = time_total // TILE
    block_total = tap_devices * lag_devices
    ext_rows = block_taps + 2 * HALO
    rows_all = dest_rows + source_count
    step_id = pl.program_id(0)
    tap_index = lax.axis_index("tap")
    time_index = lax.axis_index("tm")
    lag_index = lax.axis_index("lag")
    block_here = tap_index * lag_devices + lag_index

    def pieces(segment, block):
        for part, (block_at, source, target, size) in enumerate((
            (jnp.maximum(block - 1, 0), block_taps - HALO, 0, HALO),
            (block, 0, HALO, block_taps),
            (jnp.minimum(block + 1, block_total - 1), 0, HALO + block_taps, HALO),
        )):
            lag_step = lax.rem(lag_index - lax.rem(block_at, lag_devices) + lag_devices, lag_devices)
            tap_step = lax.rem(tap_index - lax.div(block_at, lag_devices) + tap_devices, tap_devices)
            for time_at in range(time_devices):
                time_back = lax.rem(time_index - time_at + time_devices, time_devices)
                cable_at = lag_step * time_devices + time_back

                def copy_from(
                    ref, wait=False, tap_step=tap_step, part=part, time_at=time_at,
                    source=source, target=target, size=size,
                ):
                    times = pl.ds(time_at * time_step, time_step)
                    if near:
                        raw_ref[segment, pl.ds(target, size), times] = ref[
                            tap_step, pl.ds(source, size)
                        ]
                        return
                    copy = pltpu.make_async_copy(
                        ref.at[tap_step, pl.ds(source, size)],
                        raw_ref.at[segment, pl.ds(target, size), times],
                        sems.at[segment, part * time_devices + time_at],
                    )
                    copy.wait() if wait else copy.start()

                yield cable_at, copy_from

    def start_all(segment, block):
        for cable_at, copy_from in pieces(segment, block):
            for i, ref in enumerate(cable_refs):
                pl.when(cable_at == i)(lambda ref=ref, copy_from=copy_from: copy_from(ref))

    def wait_all(segment, block):
        if not near:
            for _, copy_from in pieces(segment, block):
                copy_from(cable_refs[0], wait=True)

    @pl.when(step_id == 0)
    def prepare():
        blocks = [dest_ref[j, block_here] for j in range(dest_count)] + [block_here]
        for segment, block in enumerate(blocks):
            start_all(segment, block)
        smooth_ref[:, :LANES] = jnp.zeros((rows_all, LANES), jnp.bfloat16)
        smooth_ref[:, pl.ds(LANES + time_total, LANES)] = jnp.zeros((rows_all, LANES), jnp.bfloat16)
        for segment, block in enumerate(blocks):
            wait_all(segment, block)
            first = segment * block_taps
            rows = slice(first, first + (block_taps if segment < dest_count else source_count))
            strain = raw_ref[segment]
            smooth = jnp.dot(space_ref[0, rows], strain, preferred_element_type=jnp.float32)
            smooth = smooth + jnp.dot(
                space_ref[1, rows], strain, preferred_element_type=jnp.float32
            )
            smooth_ref[rows, pl.ds(LANES, time_total)] = smooth.astype(jnp.bfloat16)
        power = jnp.zeros((rows_all, 1), jnp.float32)
        for tile in range(tiles):
            window = smooth_ref[:, tile * TILE : tile * TILE + 2 * TILE]
            white = jnp.dot(window, time_ref[0], preferred_element_type=jnp.float32)
            white = white + jnp.dot(window, time_ref[1], preferred_element_type=jnp.float32)
            white = white.astype(jnp.bfloat16)
            bank_ref[:, tile * TILE : (tile + 1) * TILE] = white
            white = white.astype(jnp.float32)
            power = power + jnp.sum(white * white, axis=1, keepdims=True)
        energy = power / time_total + EPSILON
        inverse = jnp.broadcast_to(1.0 / jnp.sqrt(energy), (rows_all, LANES))
        scale_ref[...] = inverse[dest_rows:]
        partner_ref[...] = inverse[:dest_rows].T[:8]
        at_row = lax.broadcasted_iota(jnp.int32, (2 * TILE, TILE), 0)
        at_col = lax.broadcasted_iota(jnp.int32, (2 * TILE, TILE), 1)
        mirror = (at_row + at_col == TILE).astype(jnp.bfloat16)
        flip_ref[:, :LANES] = jnp.zeros((source_count, LANES), jnp.float32)
        blank = jnp.zeros((source_count, TILE), jnp.bfloat16)
        for tile in range(tiles + 1):
            upper = bank_ref[dest_rows:, pl.ds((tiles - tile) * TILE, TILE)] if tile else blank
            lower = bank_ref[dest_rows:, pl.ds((tiles - tile - 1) * TILE, TILE)] if tile < tiles else blank
            turned = jnp.dot(
                jnp.concatenate([lower, upper], axis=1), mirror, preferred_element_type=jnp.float32
            )
            width = TILE if tile < tiles else LANES
            flip_ref[:, pl.ds(LANES + tile * TILE, width)] = turned[:, :width]

    columns = pltpu.roll(code_ref[...], lax.rem(LANES - step_id * GROUP, LANES), 1)
    at_lane = lax.broadcasted_iota(jnp.int32, (partner_count, dest_rows), 1).astype(jnp.float32)
    hits = [at_lane == columns[:, member : member + 1] for member in range(GROUP)]

    def pick(first):
        members = slice(first, first + CHUNK)
        chosen = jnp.concatenate([hit.astype(jnp.bfloat16) for hit in hits[members]], axis=0)
        picked = jnp.dot(chosen, bank_ref[:dest_rows, :], preferred_element_type=jnp.float32)
        rows = slice(first * partner_count, (first + CHUNK) * partner_count)
        picked_ref[rows, :] = picked.astype(jnp.bfloat16)

    pick(0)
    blank = jnp.zeros((LANES, LANES), jnp.bfloat16)
    window_scale = 1.0 / (float(time_total) ** 0.5)
    first_row = step_id * GROUP
    def turned(member):
        row = flip_ref[pl.ds(first_row + member, 1), :]
        return shifted_rows(row.astype(jnp.bfloat16), LANES)

    wides = [turned(0)]
    for member in range(GROUP):
        if member % CHUNK == 0 and member + CHUNK < GROUP:
            pick(member + CHUNK)
        wide = wides[member]
        if member + 1 < GROUP:
            wides.append(turned(member + 1))

        def diagonal(k):
            if k < 0 or k > time_total // LANES:
                return blank
            start = time_total + LANES - LANES * k
            return wide[:, start : start + LANES]

        def band(first, last):
            return jnp.concatenate(
                [
                    jnp.concatenate([diagonal(k), diagonal(k - 1)], axis=1)
                    for k in range(2 * first, 2 * last)
                ],
                axis=0,
            )

        part = slice(member * partner_count, (member + 1) * partner_count)
        rows = picked_ref[part, :]
        edge = jnp.zeros((partner_count, TILE), jnp.bfloat16)
        both = jnp.dot(
            jnp.concatenate(
                [jnp.concatenate([edge, rows], axis=1), jnp.concatenate([rows, edge], axis=1)],
                axis=0,
            ),
            band(0, tiles + 1),
            preferred_element_type=jnp.float32,
        )
        before, after = both[:partner_count], both[partner_count:]
        scale = jnp.sum(
            jnp.where(hits[member], partner_ref[:1, :], 0.0), axis=1, keepdims=True
        )
        own_scale = scale_ref[pl.ds(first_row + member, 1), :] * window_scale
        scale = scale * jnp.concatenate([own_scale, own_scale], axis=1)
        out_ref[0, member, :, :TILE] = (before * scale).astype(jnp.bfloat16)
        out_ref[0, member, :, TILE:] = (after * scale).astype(jnp.bfloat16)


def per_device(raw_strain, spatial_filter, temporal_filter, dest_blocks, partner_codes):
    taps_here, time_step = raw_strain.shape
    lag_devices = lax.axis_size("lag")
    time_devices = lax.axis_size("tm")
    time_total = time_step * time_devices
    block_taps = taps_here // lag_devices
    dest_count = dest_blocks.shape[1]
    _, source_count, partner_count = partner_codes.shape
    rows_all = dest_count * block_taps + source_count
    placed = pl.BlockSpec(memory_space=pltpu.VMEM)
    bands = pl.pallas_call(
        functools.partial(bands_body, block_total=dest_blocks.shape[0]),
        grid_spec=pltpu.PrefetchScalarGridSpec(
            num_scalar_prefetch=1,
            grid=(),
            in_specs=[placed] * 3,
            out_specs=[placed] * 3,
        ),
        out_shape=[
            pltpu.VMEM((2, rows_all, block_taps + 2 * HALO), jnp.bfloat16),
            pltpu.VMEM((2, 2 * TILE, TILE), jnp.bfloat16),
            pltpu.VMEM((partner_count, LANES), jnp.float32),
        ],
    )(dest_blocks.T, partner_codes, spatial_filter, temporal_filter)
    cables, bands = gathered(raw_strain, bands)
    bands = [pltpu.with_memory_space_constraint(band, pltpu.VMEM) for band in bands]
    near = sum(cells.size for cells in cables) <= NEAR_CELLS
    if near:
        cables = [pltpu.with_memory_space_constraint(cells, pltpu.VMEM) for cells in cables]
    wide = time_total + 2 * LANES
    body = functools.partial(
        correlate_body,
        near=near,
        cable_count=len(cables),
        lag_devices=lag_devices,
        time_devices=time_devices,
    )
    return pl.pallas_call(
        body,
        grid_spec=pltpu.PrefetchScalarGridSpec(
            num_scalar_prefetch=1,
            grid=(source_count // GROUP,),
            in_specs=[placed] * 3 + [placed if near else pl.BlockSpec(memory_space=pl.ANY)] * len(cables),
            out_specs=pl.BlockSpec((1, GROUP, partner_count, LAG_COUNT), lambda i, t: (0, i, 0, 0)),
            scratch_shapes=[
                pltpu.VMEM((dest_count + 1, block_taps + 2 * HALO, time_total), jnp.bfloat16),
                pltpu.VMEM((rows_all, wide), jnp.bfloat16),
                pltpu.VMEM((rows_all, time_total), jnp.bfloat16),
                pltpu.VMEM((source_count, wide), jnp.float32),
                pltpu.VMEM((source_count, LANES), jnp.float32),
                pltpu.VMEM((8, dest_count * block_taps), jnp.float32),
                pltpu.VMEM((GROUP * partner_count, time_total), jnp.bfloat16),
                pltpu.SemaphoreType.DMA((dest_count + 1, 3 * time_devices)),
            ],
        ),
        out_shape=jax.ShapeDtypeStruct((1, source_count, partner_count, LAG_COUNT), jnp.bfloat16),
        compiler_params=pltpu.CompilerParams(vmem_limit_bytes=56 << 20),
    )(dest_blocks.T, *bands, *cables)


def solution(mesh):
    placed = (
        P(("groups", "tap"), "tm"),
        P(),
        P(),
        P("groups", None),
        P(("groups", "tap", "lag"), "tm", None),
    )
    return jax.shard_map(
        per_device,
        mesh=mesh,
        in_specs=placed,
        out_specs=P(("groups", "tap", "lag"), "tm", None, None),
        check_vma=False,
    )
```

```python
import functools

import jax
import jax.numpy as jnp
from jax import lax
from jax.experimental import pallas as pl
from jax.experimental.pallas import tpu as pltpu
from jax.sharding import PartitionSpec as P

LAG_COUNT = 512
EPSILON = 1e-06
HALO = 16
TILE = 256
LANES = 128
GROUP = 32
CHUNK = 16
NEAR_CELLS = 2 << 20


def split_parts(matrix):
    high_part = matrix.astype(jnp.bfloat16)
    low_part = (matrix - high_part.astype(jnp.float32)).astype(jnp.bfloat16)
    return high_part, low_part


def shifted_rows(row, row_count):
    wide = jnp.broadcast_to(row, (row_count, row.shape[1]))
    return pltpu.roll(wide, 0, 1, stride=1, stride_axis=0)


def gathered(raw, bands):
    lag_devices = lax.axis_size("lag")
    half_rows = raw.shape[0] // lag_devices
    half = lax.dynamic_slice_in_dim(raw, lax.axis_index("lag") * half_rows, half_rows, 0)

    def shifted(cells, axis, step):
        count = lax.axis_size(axis)
        return lax.ppermute(cells, axis, [(i, (i + step) % count) for i in range(count)])

    tap_devices = lax.axis_size("tap")
    ahead, behind = [half], [half]
    for step in range(1, tap_devices // 2 + 1):
        ahead.append(shifted(ahead[-1], "tap", 1))
        if step == 1:
            ahead[1], *bands = lax.optimization_barrier((ahead[1], *bands))
    for step in range(1, (tap_devices + 1) // 2):
        behind.append(shifted(behind[-1], "tap", tap_devices - 1))
    taps = ahead + behind[:0:-1]
    mine = [None]
    for step in range(1, lax.axis_size("tm")):
        swapped = shifted(half, "tm", step)
        if step == 1 and tap_devices > 2:
            taps[2], swapped = lax.optimization_barrier((taps[2], swapped))
        mine.append(jnp.stack([swapped] + [shifted(cells, "tm", step) for cells in taps[1:]]))
    mine[0] = jnp.stack(taps)
    cables = list(mine)
    for step in range(1, lag_devices):
        cables += [shifted(cells, "lag", step) for cells in mine]
    return cables, bands


def bands_body(dest_ref, codes_ref, space_ref, time_ref, space_out, time_out, code_out, *, block_total):
    _, source_count, partner_count = codes_ref.shape
    rows_all, ext_rows = space_out.shape[1:]
    dest_count = dest_ref.shape[0]
    block_taps = ext_rows - 2 * HALO
    tap_index = lax.axis_index("tap")
    time_index = lax.axis_index("tm")
    block_here = tap_index * lax.axis_size("lag") + lax.axis_index("lag")
    code_out[:, :source_count] = codes_ref[0].astype(jnp.float32).T
    space_row = jnp.pad(space_ref[...][None, :], ((0, 0), (0, TILE - space_ref.shape[0])))
    for segment in range(dest_count + 1):
        own = segment == dest_count
        block = block_here if own else dest_ref[segment, block_here]
        row_count = source_count if own else block_taps
        wide = shifted_rows(space_row, row_count)
        if own:
            wide = pltpu.roll(wide, time_index * source_count, 1)
        rows_at = lax.broadcasted_iota(jnp.int32, (row_count, ext_rows), 1)
        first = jnp.where(block == 0, HALO, 0)
        last = jnp.where(block == block_total - 1, HALO + block_taps, ext_rows)
        inside = jnp.logical_and(rows_at >= first, rows_at < last)
        high, low = split_parts(jnp.where(inside, wide[:, :ext_rows], 0.0))
        rows = slice(segment * block_taps, segment * block_taps + row_count)
        space_out[0, rows, :] = high
        space_out[1, rows, :] = low
    time_row = jnp.pad(time_ref[...][None, :], ((0, 0), (1, 2 * TILE - 1 - time_ref.shape[0])))
    high, low = split_parts(shifted_rows(time_row, TILE).T)
    time_out[0] = high
    time_out[1] = low


def correlate_body(*refs, near, cable_count, lag_devices, time_devices):
    dest_ref, space_ref, time_ref, code_ref = refs[:4]
    cable_refs = refs[4 : 4 + cable_count]
    out_ref, raw_ref, smooth_ref, bank_ref, flip_ref, scale_ref, partner_ref, picked_ref, sems = refs[
        4 + cable_count :
    ]
    tap_devices, block_taps, time_step = cable_refs[0].shape
    source_count, partner_count = flip_ref.shape[0], code_ref.shape[0]
    dest_count = dest_ref.shape[0]
    dest_rows = dest_count * block_taps
    time_total = time_devices * time_step
    tiles = time_total // TILE
    block_total = tap_devices * lag_devices
    ext_rows = block_taps + 2 * HALO
    rows_all = dest_rows + source_count
    step_id = pl.program_id(0)
    tap_index = lax.axis_index("tap")
    time_index = lax.axis_index("tm")
    lag_index = lax.axis_index("lag")
    block_here = tap_index * lag_devices + lag_index

    def pieces(segment, block):
        for part, (block_at, source, target, size) in enumerate((
            (jnp.maximum(block - 1, 0), block_taps - HALO, 0, HALO),
            (block, 0, HALO, block_taps),
            (jnp.minimum(block + 1, block_total - 1), 0, HALO + block_taps, HALO),
        )):
            lag_step = lax.rem(lag_index - lax.rem(block_at, lag_devices) + lag_devices, lag_devices)
            tap_step = lax.rem(tap_index - lax.div(block_at, lag_devices) + tap_devices, tap_devices)
            for time_at in range(time_devices):
                time_back = lax.rem(time_index - time_at + time_devices, time_devices)
                cable_at = lag_step * time_devices + time_back

                def copy_from(
                    ref, wait=False, tap_step=tap_step, part=part, time_at=time_at,
                    source=source, target=target, size=size,
                ):
                    times = pl.ds(time_at * time_step, time_step)
                    if near:
                        raw_ref[segment, pl.ds(target, size), times] = ref[
                            tap_step, pl.ds(source, size)
                        ]
                        return
                    copy = pltpu.make_async_copy(
                        ref.at[tap_step, pl.ds(source, size)],
                        raw_ref.at[segment, pl.ds(target, size), times],
                        sems.at[segment, part * time_devices + time_at],
                    )
                    copy.wait() if wait else copy.start()

                yield cable_at, copy_from

    def start_all(segment, block):
        for cable_at, copy_from in pieces(segment, block):
            for i, ref in enumerate(cable_refs):
                pl.when(cable_at == i)(lambda ref=ref, copy_from=copy_from: copy_from(ref))

    def wait_all(segment, block):
        if not near:
            for _, copy_from in pieces(segment, block):
                copy_from(cable_refs[0], wait=True)

    @pl.when(step_id == 0)
    def prepare():
        blocks = [dest_ref[j, block_here] for j in range(dest_count)] + [block_here]
        for segment, block in enumerate(blocks):
            start_all(segment, block)
        smooth_ref[:, :LANES] = jnp.zeros((rows_all, LANES), jnp.bfloat16)
        smooth_ref[:, pl.ds(LANES + time_total, LANES)] = jnp.zeros((rows_all, LANES), jnp.bfloat16)
        for segment, block in enumerate(blocks):
            wait_all(segment, block)
            first = segment * block_taps
            rows = slice(first, first + (block_taps if segment < dest_count else source_count))
            strain = raw_ref[segment]
            smooth = jnp.dot(space_ref[0, rows], strain, preferred_element_type=jnp.float32)
            smooth = smooth + jnp.dot(
                space_ref[1, rows], strain, preferred_element_type=jnp.float32
            )
            smooth_ref[rows, pl.ds(LANES, time_total)] = smooth.astype(jnp.bfloat16)
        power = jnp.zeros((rows_all, 1), jnp.float32)
        for tile in range(tiles):
            window = smooth_ref[:, tile * TILE : tile * TILE + 2 * TILE]
            white = jnp.dot(
                jnp.concatenate([window, window], axis=1),
                time_ref[...].reshape(4 * TILE, TILE),
                preferred_element_type=jnp.float32,
            )
            white = white.astype(jnp.bfloat16)
            bank_ref[:, tile * TILE : (tile + 1) * TILE] = white
            white = white.astype(jnp.float32)
            power = power + jnp.sum(white * white, axis=1, keepdims=True)
        energy = power / time_total + EPSILON
        inverse = jnp.broadcast_to(1.0 / jnp.sqrt(energy), (rows_all, LANES))
        scale_ref[...] = inverse[dest_rows:]
        partner_ref[...] = inverse[:dest_rows].T[:8]
        at_row = lax.broadcasted_iota(jnp.int32, (2 * TILE, TILE), 0)
        at_col = lax.broadcasted_iota(jnp.int32, (2 * TILE, TILE), 1)
        mirror = (at_row + at_col == TILE).astype(jnp.bfloat16)
        flip_ref[:, :LANES] = jnp.zeros((source_count, LANES), jnp.float32)
        blank = jnp.zeros((source_count, TILE), jnp.bfloat16)
        for tile in range(tiles + 1):
            upper = bank_ref[dest_rows:, pl.ds((tiles - tile) * TILE, TILE)] if tile else blank
            lower = bank_ref[dest_rows:, pl.ds((tiles - tile - 1) * TILE, TILE)] if tile < tiles else blank
            turned = jnp.dot(
                jnp.concatenate([lower, upper], axis=1), mirror, preferred_element_type=jnp.float32
            )
            width = TILE if tile < tiles else LANES
            flip_ref[:, pl.ds(LANES + tile * TILE, width)] = turned[:, :width]

    columns = pltpu.roll(code_ref[...], lax.rem(LANES - step_id * GROUP, LANES), 1)
    at_lane = lax.broadcasted_iota(jnp.int32, (partner_count, dest_rows), 1).astype(jnp.float32)
    hits = [at_lane == columns[:, member : member + 1] for member in range(GROUP)]

    def pick(first):
        members = slice(first, first + CHUNK)
        chosen = jnp.concatenate([hit.astype(jnp.bfloat16) for hit in hits[members]], axis=0)
        picked = jnp.dot(chosen, bank_ref[:dest_rows, :], preferred_element_type=jnp.float32)
        rows = slice(first * partner_count, (first + CHUNK) * partner_count)
        picked_ref[rows, :] = picked.astype(jnp.bfloat16)

    pick(0)
    blank = jnp.zeros((LANES, LANES), jnp.bfloat16)
    window_scale = 1.0 / (float(time_total) ** 0.5)
    first_row = step_id * GROUP
    def turned(member):
        row = flip_ref[pl.ds(first_row + member, 1), :]
        return shifted_rows(row.astype(jnp.bfloat16), LANES)

    wides = [turned(0)]
    for member in range(GROUP):
        if member % CHUNK == 0 and member + CHUNK < GROUP:
            pick(member + CHUNK)
        wide = wides[member]
        if member + 1 < GROUP:
            wides.append(turned(member + 1))

        def diagonal(k):
            if k < 0 or k > time_total // LANES:
                return blank
            start = time_total + LANES - LANES * k
            return wide[:, start : start + LANES]

        def band(first, last):
            return jnp.concatenate(
                [
                    jnp.concatenate([diagonal(k), diagonal(k - 1)], axis=1)
                    for k in range(2 * first, 2 * last)
                ],
                axis=0,
            )

        part = slice(member * partner_count, (member + 1) * partner_count)
        rows = picked_ref[part, :]
        edge = jnp.zeros((partner_count, TILE), jnp.bfloat16)
        both = jnp.dot(
            jnp.concatenate(
                [jnp.concatenate([edge, rows], axis=1), jnp.concatenate([rows, edge], axis=1)],
                axis=0,
            ),
            band(0, tiles + 1),
            preferred_element_type=jnp.float32,
        )
        before, after = both[:partner_count], both[partner_count:]
        scale = jnp.sum(
            jnp.where(hits[member], partner_ref[:1, :], 0.0), axis=1, keepdims=True
        )
        own_scale = scale_ref[pl.ds(first_row + member, 1), :] * window_scale
        scale = scale * jnp.concatenate([own_scale, own_scale], axis=1)
        out_ref[0, member, :, :TILE] = (before * scale).astype(jnp.bfloat16)
        out_ref[0, member, :, TILE:] = (after * scale).astype(jnp.bfloat16)


def per_device(raw_strain, spatial_filter, temporal_filter, dest_blocks, partner_codes):
    taps_here, time_step = raw_strain.shape
    lag_devices = lax.axis_size("lag")
    time_devices = lax.axis_size("tm")
    time_total = time_step * time_devices
    block_taps = taps_here // lag_devices
    dest_count = dest_blocks.shape[1]
    _, source_count, partner_count = partner_codes.shape
    rows_all = dest_count * block_taps + source_count
    placed = pl.BlockSpec(memory_space=pltpu.VMEM)
    bands = pl.pallas_call(
        functools.partial(bands_body, block_total=dest_blocks.shape[0]),
        grid_spec=pltpu.PrefetchScalarGridSpec(
            num_scalar_prefetch=1,
            grid=(),
            in_specs=[placed] * 3,
            out_specs=[placed] * 3,
        ),
        out_shape=[
            pltpu.VMEM((2, rows_all, block_taps + 2 * HALO), jnp.bfloat16),
            pltpu.VMEM((2, 2 * TILE, TILE), jnp.bfloat16),
            pltpu.VMEM((partner_count, LANES), jnp.float32),
        ],
    )(dest_blocks.T, partner_codes, spatial_filter, temporal_filter)
    cables, bands = gathered(raw_strain, bands)
    bands = [pltpu.with_memory_space_constraint(band, pltpu.VMEM) for band in bands]
    near = sum(cells.size for cells in cables) <= NEAR_CELLS
    if near:
        cables = [pltpu.with_memory_space_constraint(cells, pltpu.VMEM) for cells in cables]
    wide = time_total + 2 * LANES
    body = functools.partial(
        correlate_body,
        near=near,
        cable_count=len(cables),
        lag_devices=lag_devices,
        time_devices=time_devices,
    )
    return pl.pallas_call(
        body,
        grid_spec=pltpu.PrefetchScalarGridSpec(
            num_scalar_prefetch=1,
            grid=(source_count // GROUP,),
            in_specs=[placed] * 3 + [placed if near else pl.BlockSpec(memory_space=pl.ANY)] * len(cables),
            out_specs=pl.BlockSpec((1, GROUP, partner_count, LAG_COUNT), lambda i, t: (0, i, 0, 0)),
            scratch_shapes=[
                pltpu.VMEM((dest_count + 1, block_taps + 2 * HALO, time_total), jnp.bfloat16),
                pltpu.VMEM((rows_all, wide), jnp.bfloat16),
                pltpu.VMEM((rows_all, time_total), jnp.bfloat16),
                pltpu.VMEM((source_count, wide), jnp.float32),
                pltpu.VMEM((source_count, LANES), jnp.float32),
                pltpu.VMEM((8, dest_count * block_taps), jnp.float32),
                pltpu.VMEM((GROUP * partner_count, time_total), jnp.bfloat16),
                pltpu.SemaphoreType.DMA((dest_count + 1, 3 * time_devices)),
            ],
        ),
        out_shape=jax.ShapeDtypeStruct((1, source_count, partner_count, LAG_COUNT), jnp.bfloat16),
        compiler_params=pltpu.CompilerParams(vmem_limit_bytes=56 << 20),
    )(dest_blocks.T, *bands, *cables)


def solution(mesh):
    placed = (
        P(("groups", "tap"), "tm"),
        P(),
        P(),
        P("groups", None),
        P(("groups", "tap", "lag"), "tm", None),
    )
    return jax.shard_map(
        per_device,
        mesh=mesh,
        in_specs=placed,
        out_specs=P(("groups", "tap", "lag"), "tm", None, None),
        check_vma=False,
    )
```

```python
import functools

import jax
import jax.numpy as jnp
from jax import lax
from jax.experimental import pallas as pl
from jax.experimental.pallas import tpu as pltpu
from jax.sharding import PartitionSpec as P

LAG_COUNT = 512
EPSILON = 1e-06
HALO = 16
TILE = 256
LANES = 128
GROUP = 32
CHUNK = 8
NEAR_CELLS = 2 << 20


def split_parts(matrix):
    high_part = matrix.astype(jnp.bfloat16)
    low_part = (matrix - high_part.astype(jnp.float32)).astype(jnp.bfloat16)
    return high_part, low_part


def shifted_rows(row, row_count):
    wide = jnp.broadcast_to(row, (row_count, row.shape[1]))
    return pltpu.roll(wide, 0, 1, stride=1, stride_axis=0)


def gathered(raw, bands):
    lag_devices = lax.axis_size("lag")
    half_rows = raw.shape[0] // lag_devices
    half = lax.dynamic_slice_in_dim(raw, lax.axis_index("lag") * half_rows, half_rows, 0)

    def shifted(cells, axis, step):
        count = lax.axis_size(axis)
        return lax.ppermute(cells, axis, [(i, (i + step) % count) for i in range(count)])

    tap_devices = lax.axis_size("tap")
    ahead, behind = [half], [half]
    for step in range(1, tap_devices // 2 + 1):
        ahead.append(shifted(ahead[-1], "tap", 1))
        if step == 1:
            ahead[1], *bands = lax.optimization_barrier((ahead[1], *bands))
    for step in range(1, (tap_devices + 1) // 2):
        behind.append(shifted(behind[-1], "tap", tap_devices - 1))
    taps = ahead + behind[:0:-1]
    mine = [None]
    for step in range(1, lax.axis_size("tm")):
        swapped = shifted(half, "tm", step)
        if step == 1 and tap_devices > 2:
            taps[2], swapped = lax.optimization_barrier((taps[2], swapped))
        mine.append(jnp.stack([swapped] + [shifted(cells, "tm", step) for cells in taps[1:]]))
    mine[0] = jnp.stack(taps)
    cables = list(mine)
    for step in range(1, lag_devices):
        cables += [shifted(cells, "lag", step) for cells in mine]
    return cables, bands


def bands_body(dest_ref, codes_ref, space_ref, time_ref, space_out, time_out, code_out, *, block_total):
    _, source_count, partner_count = codes_ref.shape
    rows_all, ext_rows = space_out.shape[1:]
    dest_count = dest_ref.shape[0]
    block_taps = ext_rows - 2 * HALO
    tap_index = lax.axis_index("tap")
    time_index = lax.axis_index("tm")
    block_here = tap_index * lax.axis_size("lag") + lax.axis_index("lag")
    code_out[:, :source_count] = codes_ref[0].astype(jnp.float32).T
    space_row = jnp.pad(space_ref[...][None, :], ((0, 0), (0, TILE - space_ref.shape[0])))
    for segment in range(dest_count + 1):
        own = segment == dest_count
        block = block_here if own else dest_ref[segment, block_here]
        row_count = source_count if own else block_taps
        wide = shifted_rows(space_row, row_count)
        if own:
            wide = pltpu.roll(wide, time_index * source_count, 1)
        rows_at = lax.broadcasted_iota(jnp.int32, (row_count, ext_rows), 1)
        first = jnp.where(block == 0, HALO, 0)
        last = jnp.where(block == block_total - 1, HALO + block_taps, ext_rows)
        inside = jnp.logical_and(rows_at >= first, rows_at < last)
        high, low = split_parts(jnp.where(inside, wide[:, :ext_rows], 0.0))
        rows = slice(segment * block_taps, segment * block_taps + row_count)
        space_out[0, rows, :] = high
        space_out[1, rows, :] = low
    time_row = jnp.pad(time_ref[...][None, :], ((0, 0), (1, 2 * TILE - 1 - time_ref.shape[0])))
    high, low = split_parts(shifted_rows(time_row, TILE).T)
    time_out[0] = high
    time_out[1] = low


def correlate_body(*refs, near, cable_count, lag_devices, time_devices):
    dest_ref, space_ref, time_ref, code_ref = refs[:4]
    cable_refs = refs[4 : 4 + cable_count]
    out_ref, raw_ref, smooth_ref, bank_ref, flip_ref, scale_ref, partner_ref, picked_ref, sems = refs[
        4 + cable_count :
    ]
    tap_devices, block_taps, time_step = cable_refs[0].shape
    source_count, partner_count = flip_ref.shape[0], code_ref.shape[0]
    dest_count = dest_ref.shape[0]
    dest_rows = dest_count * block_taps
    time_total = time_devices * time_step
    tiles = time_total // TILE
    block_total = tap_devices * lag_devices
    ext_rows = block_taps + 2 * HALO
    rows_all = dest_rows + source_count
    step_id = pl.program_id(0)
    tap_index = lax.axis_index("tap")
    time_index = lax.axis_index("tm")
    lag_index = lax.axis_index("lag")
    block_here = tap_index * lag_devices + lag_index

    def pieces(segment, block):
        for part, (block_at, source, target, size) in enumerate((
            (jnp.maximum(block - 1, 0), block_taps - HALO, 0, HALO),
            (block, 0, HALO, block_taps),
            (jnp.minimum(block + 1, block_total - 1), 0, HALO + block_taps, HALO),
        )):
            lag_step = lax.rem(lag_index - lax.rem(block_at, lag_devices) + lag_devices, lag_devices)
            tap_step = lax.rem(tap_index - lax.div(block_at, lag_devices) + tap_devices, tap_devices)
            for time_at in range(time_devices):
                time_back = lax.rem(time_index - time_at + time_devices, time_devices)
                cable_at = lag_step * time_devices + time_back

                def copy_from(
                    ref, wait=False, tap_step=tap_step, part=part, time_at=time_at,
                    source=source, target=target, size=size,
                ):
                    times = pl.ds(time_at * time_step, time_step)
                    if near:
                        raw_ref[segment, pl.ds(target, size), times] = ref[
                            tap_step, pl.ds(source, size)
                        ]
                        return
                    copy = pltpu.make_async_copy(
                        ref.at[tap_step, pl.ds(source, size)],
                        raw_ref.at[segment, pl.ds(target, size), times],
                        sems.at[segment, part * time_devices + time_at],
                    )
                    copy.wait() if wait else copy.start()

                yield cable_at, copy_from

    def start_all(segment, block):
        for cable_at, copy_from in pieces(segment, block):
            for i, ref in enumerate(cable_refs):
                pl.when(cable_at == i)(lambda ref=ref, copy_from=copy_from: copy_from(ref))

    def wait_all(segment, block):
        if not near:
            for _, copy_from in pieces(segment, block):
                copy_from(cable_refs[0], wait=True)

    @pl.when(step_id == 0)
    def prepare():
        blocks = [dest_ref[j, block_here] for j in range(dest_count)] + [block_here]
        for segment, block in enumerate(blocks):
            start_all(segment, block)
        smooth_ref[:, :LANES] = jnp.zeros((rows_all, LANES), jnp.bfloat16)
        smooth_ref[:, pl.ds(LANES + time_total, LANES)] = jnp.zeros((rows_all, LANES), jnp.bfloat16)
        for segment, block in enumerate(blocks):
            wait_all(segment, block)
            first = segment * block_taps
            rows = slice(first, first + (block_taps if segment < dest_count else source_count))
            strain = raw_ref[segment]
            smooth = jnp.dot(space_ref[0, rows], strain, preferred_element_type=jnp.float32)
            smooth = smooth + jnp.dot(
                space_ref[1, rows], strain, preferred_element_type=jnp.float32
            )
            smooth_ref[rows, pl.ds(LANES, time_total)] = smooth.astype(jnp.bfloat16)
        power = jnp.zeros((rows_all, 1), jnp.float32)
        for tile in range(tiles):
            window = smooth_ref[:, tile * TILE : tile * TILE + 2 * TILE]
            white = jnp.dot(window, time_ref[0], preferred_element_type=jnp.float32)
            white = white + jnp.dot(window, time_ref[1], preferred_element_type=jnp.float32)
            white = white.astype(jnp.bfloat16)
            bank_ref[:, tile * TILE : (tile + 1) * TILE] = white
            white = white.astype(jnp.float32)
            power = power + jnp.sum(white * white, axis=1, keepdims=True)
        energy = power / time_total + EPSILON
        inverse = jnp.broadcast_to(1.0 / jnp.sqrt(energy), (rows_all, LANES))
        scale_ref[...] = inverse[dest_rows:]
        partner_ref[...] = inverse[:dest_rows].T[:8]
        at_row = lax.broadcasted_iota(jnp.int32, (2 * TILE, TILE), 0)
        at_col = lax.broadcasted_iota(jnp.int32, (2 * TILE, TILE), 1)
        mirror = (at_row + at_col == TILE).astype(jnp.bfloat16)
        flip_ref[:, :LANES] = jnp.zeros((source_count, LANES), jnp.float32)
        blank = jnp.zeros((source_count, TILE), jnp.bfloat16)
        for tile in range(tiles + 1):
            upper = bank_ref[dest_rows:, pl.ds((tiles - tile) * TILE, TILE)] if tile else blank
            lower = bank_ref[dest_rows:, pl.ds((tiles - tile - 1) * TILE, TILE)] if tile < tiles else blank
            turned = jnp.dot(
                jnp.concatenate([lower, upper], axis=1), mirror, preferred_element_type=jnp.float32
            )
            width = TILE if tile < tiles else LANES
            flip_ref[:, pl.ds(LANES + tile * TILE, width)] = turned[:, :width]

    columns = pltpu.roll(code_ref[...], lax.rem(LANES - step_id * GROUP, LANES), 1)
    at_lane = lax.broadcasted_iota(jnp.int32, (partner_count, dest_rows), 1).astype(jnp.float32)
    hits = [at_lane == columns[:, member : member + 1] for member in range(GROUP)]

    def pick(first):
        members = slice(first, first + CHUNK)
        chosen = jnp.concatenate([hit.astype(jnp.bfloat16) for hit in hits[members]], axis=0)
        picked = jnp.dot(chosen, bank_ref[:dest_rows, :], preferred_element_type=jnp.float32)
        rows = slice(first * partner_count, (first + CHUNK) * partner_count)
        picked_ref[rows, :] = picked.astype(jnp.bfloat16)

    pick(0)
    blank = jnp.zeros((LANES, LANES), jnp.bfloat16)
    window_scale = 1.0 / (float(time_total) ** 0.5)
    first_row = step_id * GROUP
    for member in range(GROUP):
        if member % CHUNK == 0 and member + CHUNK < GROUP:
            pick(member + CHUNK)
        row = flip_ref[pl.ds(first_row + member, 1), :]
        wide = shifted_rows(row.astype(jnp.bfloat16), LANES)

        def diagonal(k):
            if k < 0 or k > time_total // LANES:
                return blank
            start = time_total + LANES - LANES * k
            return wide[:, start : start + LANES]

        def band(first, last):
            return jnp.concatenate(
                [
                    jnp.concatenate([diagonal(k), diagonal(k - 1)], axis=1)
                    for k in range(2 * first, 2 * last)
                ],
                axis=0,
            )

        part = slice(member * partner_count, (member + 1) * partner_count)
        rows = picked_ref[part, :]
        edge = jnp.zeros((partner_count, TILE), jnp.bfloat16)
        both = jnp.dot(
            jnp.concatenate(
                [jnp.concatenate([edge, rows], axis=1), jnp.concatenate([rows, edge], axis=1)],
                axis=0,
            ),
            band(0, tiles + 1),
            preferred_element_type=jnp.float32,
        )
        before, after = both[:partner_count], both[partner_count:]
        scale = jnp.sum(
            jnp.where(hits[member], partner_ref[:1, :], 0.0), axis=1, keepdims=True
        )
        own_scale = scale_ref[pl.ds(first_row + member, 1), :] * window_scale
        scale = scale * jnp.concatenate([own_scale, own_scale], axis=1)
        out_ref[0, member, :, :TILE] = (before * scale).astype(jnp.bfloat16)
        out_ref[0, member, :, TILE:] = (after * scale).astype(jnp.bfloat16)


def per_device(raw_strain, spatial_filter, temporal_filter, dest_blocks, partner_codes):
    taps_here, time_step = raw_strain.shape
    lag_devices = lax.axis_size("lag")
    time_devices = lax.axis_size("tm")
    time_total = time_step * time_devices
    block_taps = taps_here // lag_devices
    dest_count = dest_blocks.shape[1]
    _, source_count, partner_count = partner_codes.shape
    rows_all = dest_count * block_taps + source_count
    placed = pl.BlockSpec(memory_space=pltpu.VMEM)
    bands = pl.pallas_call(
        functools.partial(bands_body, block_total=dest_blocks.shape[0]),
        grid_spec=pltpu.PrefetchScalarGridSpec(
            num_scalar_prefetch=1,
            grid=(),
            in_specs=[placed] * 3,
            out_specs=[placed] * 3,
        ),
        out_shape=[
            pltpu.VMEM((2, rows_all, block_taps + 2 * HALO), jnp.bfloat16),
            pltpu.VMEM((2, 2 * TILE, TILE), jnp.bfloat16),
            pltpu.VMEM((partner_count, LANES), jnp.float32),
        ],
    )(dest_blocks.T, partner_codes, spatial_filter, temporal_filter)
    cables, bands = gathered(raw_strain, bands)
    bands = [pltpu.with_memory_space_constraint(band, pltpu.VMEM) for band in bands]
    near = sum(cells.size for cells in cables) <= NEAR_CELLS
    if near:
        cables = [pltpu.with_memory_space_constraint(cells, pltpu.VMEM) for cells in cables]
    wide = time_total + 2 * LANES
    body = functools.partial(
        correlate_body,
        near=near,
        cable_count=len(cables),
        lag_devices=lag_devices,
        time_devices=time_devices,
    )
    return pl.pallas_call(
        body,
        grid_spec=pltpu.PrefetchScalarGridSpec(
            num_scalar_prefetch=1,
            grid=(source_count // GROUP,),
            in_specs=[placed] * 3 + [placed if near else pl.BlockSpec(memory_space=pl.ANY)] * len(cables),
            out_specs=pl.BlockSpec((1, GROUP, partner_count, LAG_COUNT), lambda i, t: (0, i, 0, 0)),
            scratch_shapes=[
                pltpu.VMEM((dest_count + 1, block_taps + 2 * HALO, time_total), jnp.bfloat16),
                pltpu.VMEM((rows_all, wide), jnp.bfloat16),
                pltpu.VMEM((rows_all, time_total), jnp.bfloat16),
                pltpu.VMEM((source_count, wide), jnp.float32),
                pltpu.VMEM((source_count, LANES), jnp.float32),
                pltpu.VMEM((8, dest_count * block_taps), jnp.float32),
                pltpu.VMEM((GROUP * partner_count, time_total), jnp.bfloat16),
                pltpu.SemaphoreType.DMA((dest_count + 1, 3 * time_devices)),
            ],
        ),
        out_shape=jax.ShapeDtypeStruct((1, source_count, partner_count, LAG_COUNT), jnp.bfloat16),
        compiler_params=pltpu.CompilerParams(vmem_limit_bytes=56 << 20),
    )(dest_blocks.T, *bands, *cables)


def solution(mesh):
    placed = (
        P(("groups", "tap"), "tm"),
        P(),
        P(),
        P("groups", None),
        P(("groups", "tap", "lag"), "tm", None),
    )
    return jax.shard_map(
        per_device,
        mesh=mesh,
        in_specs=placed,
        out_specs=P(("groups", "tap", "lag"), "tm", None, None),
        check_vma=False,
    )
```
